256 devices in a mesh: tm: 32 (over x_hi, z, core), stripe: 8 (over x_lo, y).
Axes of the slice: x: 4 (x_hi: 2, x_lo: 2; x = x_hi * 2 + x_lo), y: 4, z: 8, core: 2. Of those that a mesh axis runs over, the one named last changes fastest.
Arguments:
- data_vec: float32 [128, 2, 512], P('tm', None, 'stripe'), may hold values from -6 to 6
- kernel: bfloat16 [128, 2, 512, 8192], P('tm', None, None, 'stripe'), may hold values from -0.1875 to 0.1875
- time_spectrum: float32 [128], P('tm'), may hold values from 0.25 to 2
- prior_spectrum: float32 [128, 64], replicated, may hold values from 0.05 to 1
- noise_var: float32 [512], P('stripe'), may hold values from 0.1 to 1
Outputs:
- hessian_vec: float32 [128, 2, 512], P('tm', None, 'stripe')
The draws below stay inside these ranges and needn't reach their ends.
All inputs are finite; a program needn't handle non-finite values.
Results may differ from the reference program's by a relative error of at most 0.0022.
Values may be sent and summed in bfloat16 or wider, within the bound.
No kernel may reach another device: no remote copies, remote signals or barrier semaphores. Data moves between devices by JAX's collectives and lax.ppermute only.
A program may use at most 64 MiB of HBM per device.

```python
import math
import jax
import jax.numpy as jnp
from jax import lax

NS = 512
G1 = 128
G2 = 64
NT = 128
NV = 2
NF = 128
NP = 8192


def levels(stream_key, extent, shards, smallest, high):
    def one(position, blocks):
        steps = jax.random.uniform(jax.random.fold_in(jax.random.fold_in(stream_key, 6), position), (blocks,), jnp.float32, smallest / len(shards), high / len(shards))
        return jnp.repeat(jnp.exp(steps), extent[position] // blocks).reshape((-1,) + (1,) * (len(extent) - position - 1))

    factor_of = one(*shards[0])
    for cut in shards[1:]:
        factor_of = factor_of * one(*cut)
    return factor_of


def scatter_about(key, extent, width, most, cuts=(), held_as=jnp.bfloat16):
    result = jax.random.normal(key, extent, jnp.float32) * width
    if len(cuts) > 0:
        result = levels(key, extent, cuts, -0.22, 0.18) * result
    return jnp.clip(result, min=-most, max=most).astype(held_as)


def setup_inputs(seed: int = 0) -> dict:
    splits = jax.random.split(jax.random.key(seed), 6)
    data_vec = scatter_about(splits[0], (NT, NV, NS), 1.0, 6.0, ((0, 32), (2, 8)), jnp.float32)
    kernel = scatter_about(splits[1], (NF, 2, NS, NP), (2 * NS) ** -0.5, 0.1875, ((0, 32), (3, 8)))
    time_spectrum = jnp.clip(jnp.exp(math.log(2.0) - 2.0794415 * jax.random.uniform(splits[2], (NF,), jnp.float32) ** levels(splits[2], (NF,), ((0, 32),), -0.2, 0.2)), 0.25, 2.0)
    prior_spectrum = jnp.clip(jnp.exp(jax.random.uniform(splits[3], (G1, G2), jnp.float32, math.log(0.05), math.log(1.0))), 0.05, 1.0)
    noise_var = jnp.clip(jnp.exp(math.log(1.0) - 2.3025851 * jax.random.uniform(splits[4], (NS,), jnp.float32) ** levels(splits[4], (NS,), ((0, 8),), -0.2, 0.2)), 0.1, 1.0)
    return {"data_vec": data_vec, "kernel": kernel, "time_spectrum": time_spectrum, "prior_spectrum": prior_spectrum, "noise_var": noise_var}


precise = lax.Precision.HIGHEST

def angle_tables(freq_ids, time_ids, length):
    product = freq_ids[:, None] * time_ids[None, :] % (2 * length)
    angles = product.astype(jnp.float32) * (math.pi / length)
    return (jnp.cos(angles), jnp.sin(angles))

def sine_matrix(length):
    numbers = jnp.arange(length, dtype=jnp.int32) + 1
    product = numbers[:, None] * numbers[None, :] % (2 * (length + 1))
    return jnp.sin(product.astype(jnp.float32) * (math.pi / (length + 1))) * math.sqrt(2.0 / (length + 1))

def reference(data_vec, kernel, time_spectrum, prior_spectrum, noise_var):
    numbers = jnp.arange(NT, dtype=jnp.int32)
    cosine, sine_part = angle_tables(numbers, numbers, NT)
    flattened = data_vec.reshape(NT, NV * NS)
    real_part = jnp.dot(cosine, flattened, precision=precise) / math.sqrt(NT)
    imag_part = -jnp.dot(sine_part, flattened, precision=precise) / math.sqrt(NT)
    spectra = jnp.stack([real_part, imag_part], 1).reshape(NF, 2, NV, NS).astype(jnp.bfloat16)
    row_sine = sine_matrix(G1)
    column_sine = sine_matrix(G2)

    def one_freq(packed):
        spectrum, weights, freq_scale = packed
        adj_real = jnp.dot(spectrum[0], weights[0], preferred_element_type=jnp.float32) + jnp.dot(spectrum[1], weights[1], preferred_element_type=jnp.float32)
        adj_imag = jnp.dot(spectrum[1], weights[0], preferred_element_type=jnp.float32) - jnp.dot(spectrum[0], weights[1], preferred_element_type=jnp.float32)
        adjoint = jnp.stack([adj_real, adj_imag]) * freq_scale
        grid_stack = adjoint.reshape(2 * NV, G1, G2)
        forward_grid = jnp.einsum('ai,mij->maj', row_sine, grid_stack, precision=precise)
        forward_grid = jnp.einsum('maj,jb->mab', forward_grid, column_sine, precision=precise) * prior_spectrum
        backward_grid = jnp.einsum('ia,mab->mib', row_sine, forward_grid, precision=precise)
        backward_grid = jnp.einsum('mib,bj->mij', backward_grid, column_sine, precision=precise)
        smoothed = backward_grid.reshape(2, NV, NP).astype(jnp.bfloat16)
        out_real = jnp.dot(smoothed[0], weights[0].T, preferred_element_type=jnp.float32) - jnp.dot(smoothed[1], weights[1].T, preferred_element_type=jnp.float32)
        out_imag = jnp.dot(smoothed[1], weights[0].T, preferred_element_type=jnp.float32) + jnp.dot(smoothed[0], weights[1].T, preferred_element_type=jnp.float32)
        return jnp.stack([out_real, out_imag])
    images = lax.map(one_freq, (spectra, kernel, time_spectrum))
    time_real = jnp.einsum('kt,kns->tns', cosine, images[:, 0], precision=precise)
    time_imag = jnp.einsum('kt,kns->tns', sine_part, images[:, 1], precision=precise)
    return (time_real - time_imag) / math.sqrt(NT) + noise_var[None, None, :] * data_vec
```

```python
import functools
import math

import jax
import jax.numpy as jnp
import numpy as np
from jax import lax
from jax.experimental import pallas as pl
from jax.experimental.pallas import tpu as pltpu
from jax.sharding import PartitionSpec as P

exact = lax.Precision.HIGHEST
f32 = jnp.float32
bf16 = jnp.bfloat16


def whole():
    return pl.BlockSpec(memory_space=pltpu.VMEM)


def scalars():
    return pl.BlockSpec(memory_space=pltpu.SMEM)


def call(body, out_shape, operands, specs, scratch=()):
    return pl.pallas_call(
        body,
        out_shape=out_shape,
        in_specs=list(specs),
        out_specs=whole(),
        scratch_shapes=list(scratch),
    )(*operands)


def mm(a, b, dims=((1,), (0,)), precision=exact):
    return lax.dot_general(
        a, b, (dims, ((), ())), precision=precision, preferred_element_type=f32
    )


def fourier_table(blocks):
    steps = np.arange(128)
    angles = np.outer(steps, steps) % 256 * (math.pi / 128)
    pair = np.stack([np.cos(angles), -np.sin(angles)]) / math.sqrt(128)
    pair = pair.reshape(2, blocks, 128 // blocks, 128).transpose(1, 0, 2, 3)
    return pair.reshape(blocks, 2 * (128 // blocks), 128).astype(np.float32)


def sine_matrix(length):
    numbers = np.arange(length) + 1
    product = np.outer(numbers, numbers) % (2 * (length + 1))
    return np.sin(product * (math.pi / (length + 1))) * math.sqrt(2.0 / (length + 1))


def row_order():
    stripe, parity, c = np.meshgrid(np.arange(8), np.arange(2), np.arange(8), indexing="ij")
    return (stripe * 16 + 2 * c + parity).reshape(-1)


def low_half(shape):
    return lax.broadcasted_iota(jnp.int32, shape, len(shape) - 1) < 64


def swap_halves(first, second):
    keep = low_half(first.shape)
    low = jnp.where(keep, first, pltpu.roll(second, 64, 1))
    high = jnp.where(keep, pltpu.roll(first, 64, 1), second)
    return low, high


def spread_body(data_ref, out_ref):
    flat = jnp.concatenate([data_ref[:, 0, :], data_ref[:, 1, :]], axis=1)
    two = jnp.concatenate([flat, flat], axis=0)
    for r in range(16):
        out_ref[r * 8 : r * 8 + 8, :] = two


def spectra_body(data_ref, table_ref, out_ref):
    tm = lax.axis_index("tm")
    spectra = mm(table_ref[tm], data_ref[...]).astype(bf16)
    for r in range(8):
        out_ref[r] = spectra


def adjoint_body(gathered_ref, kernel_ref, scale_ref, column_ref, out_ref, grid_ref):
    parts = [[], []]
    for j in range(4):
        first = gathered_ref[2 * j].astype(f32)
        second = gathered_ref[2 * j + 1].astype(f32)
        low, high = swap_halves(first, second)
        parts[0].append(low)
        parts[1].append(high)
    rows = [jnp.concatenate(part, axis=1) for part in parts]
    sub = lax.broadcasted_iota(jnp.int32, (8, 512), 0)
    turned = [jnp.where(sub < 4, pltpu.roll(r, 4, 0), -pltpu.roll(r, 4, 0)) for r in rows]
    straight = jnp.concatenate(rows, axis=0)
    turned = jnp.concatenate(turned, axis=0)
    freq = lax.broadcasted_iota(jnp.int32, (16, 512), 0) % 4
    total = None
    for k in range(4):
        for c, source in enumerate((straight, turned)):
            left = jnp.where(freq == k, source, 0.0).astype(bf16)
            term = mm(left, kernel_ref[k, c], precision=None)
            total = term if total is None else total + term
    row = lax.broadcasted_iota(jnp.int32, (16, 1024), 0) % 4
    scale = jnp.where(
        row < 2,
        jnp.where(row == 0, scale_ref[0], scale_ref[1]),
        jnp.where(row == 2, scale_ref[2], scale_ref[3]),
    )
    total = total * scale
    stack = jnp.concatenate([total[:, c * 128 : c * 128 + 128] for c in range(8)], axis=0)
    grid_ref[...] = mm(stack, column_ref[...])
    for m in range(8):
        first = grid_ref[pl.ds(2 * m, 8, stride=16), :]
        second = grid_ref[pl.ds(2 * m + 1, 8, stride=16), :]
        low, high = swap_halves(first, second)
        for r in range(8):
            out_ref[r, 0:8, m * 128 : m * 128 + 128] = low
            out_ref[r, 8:16, m * 128 : m * 128 + 128] = high


def images_body(
    grids_ref, kernel_ref, prior_ref, forward_ref, backward_ref, column_ref, out_ref, grid_ref
):
    stripe = lax.axis_index("stripe")
    modes = mm(forward_ref[...], grids_ref[...])
    prior = prior_ref[...].T
    prior = jnp.concatenate([prior, prior], axis=1)
    modes = modes * jnp.concatenate([prior] * 8, axis=1)
    back = mm(backward_ref[pl.ds(stripe * 16, 16), :], modes)
    for m in range(8):
        first, second = swap_halves(
            back[0:8, m * 128 : m * 128 + 128], back[8:16, m * 128 : m * 128 + 128]
        )
        grid_ref[pl.ds(2 * m, 8, stride=16), :] = first
        grid_ref[pl.ds(2 * m + 1, 8, stride=16), :] = second
    smooth = mm(grid_ref[...], column_ref[...])
    smooth = jnp.concatenate([smooth[c * 16 : c * 16 + 16, :] for c in range(8)], axis=1)
    sub = lax.broadcasted_iota(jnp.int32, (8, 1024), 0)
    turned = []
    for n in range(2):
        moved = pltpu.roll(smooth[n * 8 : n * 8 + 8, :], 4, 0)
        turned.append(jnp.where(sub < 4, -moved, moved))
    turned = jnp.concatenate(turned, axis=0)
    freq = lax.broadcasted_iota(jnp.int32, (16, 1024), 0) % 4
    total = None
    for k in range(4):
        for c, source in enumerate((smooth, turned)):
            left = jnp.where(freq == k, source, 0.0).astype(bf16)
            term = mm(left, kernel_ref[k, c], ((1,), (1,)), precision=None)
            total = term if total is None else total + term
    for j in range(4):
        low, high = swap_halves(
            total[0:8, j * 128 : j * 128 + 128], total[8:16, j * 128 : j * 128 + 128]
        )
        out_ref[2 * j] = low
        out_ref[2 * j + 1] = high


def times_body(images_ref, table_ref, out_ref):
    tm = lax.axis_index("tm")
    total = images_ref[0]
    for r in range(1, 8):
        total = total + images_ref[r]
    out_ref[...] = mm(table_ref[tm], total, ((0,), (0,)))


def finish_body(sums_ref, data_ref, noise_ref, out_ref):
    total = sums_ref[0:8, :]
    for r in range(1, 16):
        total = total + sums_ref[r * 8 : r * 8 + 8, :]
    total = total[0:4, :] + total[4:8, :]
    noise = noise_ref[...]
    out_ref[:, 0, :] = total[:, 0:64] + noise * data_ref[:, 0, :]
    out_ref[:, 1, :] = total[:, 64:128] + noise * data_ref[:, 1, :]


def exchange(x, axis):
    return lax.all_to_all(x, axis, 0, 0, tiled=True)


def shards(data_vec, kernel, time_spectrum, prior_spectrum, noise_var):
    table = jnp.asarray(fourier_table(32))
    rows = sine_matrix(128)
    order = row_order()
    backward = jnp.asarray(rows[order].astype(np.float32))
    forward = jnp.asarray(rows[:, order].astype(np.float32))
    columns = sine_matrix(64)
    column = jnp.asarray(np.kron(np.eye(2), columns).astype(np.float32))

    spread = call(spread_body, jax.ShapeDtypeStruct((128, 128), f32), (data_vec,), (whole(),))
    by_time = exchange(spread.reshape(32, 4, 128), "tm").reshape(128, 128)
    spectra = call(
        spectra_body,
        jax.ShapeDtypeStruct((8, 8, 128), bf16),
        (by_time, table),
        (whole(), whole()),
    )
    gathered = exchange(spectra, "stripe")
    grids = call(
        adjoint_body,
        jax.ShapeDtypeStruct((8, 16, 1024), f32),
        (gathered, kernel, time_spectrum, column),
        (whole(), whole(), scalars(), whole()),
        (pltpu.VMEM((128, 128), f32),),
    )
    grids = exchange(grids, "stripe").reshape(128, 1024)
    images = call(
        images_body,
        jax.ShapeDtypeStruct((8, 8, 128), f32),
        (grids, kernel, prior_spectrum.T, forward, backward, column),
        (whole(),) * 6,
        (pltpu.VMEM((128, 128), f32),),
    )
    images = exchange(images, "stripe")
    sums = call(
        times_body, jax.ShapeDtypeStruct((128, 128), f32), (images, table), (whole(), whole())
    )
    sums = exchange(sums.reshape(32, 4, 128), "tm").reshape(128, 128)
    return call(
        finish_body,
        jax.ShapeDtypeStruct((4, 2, 64), f32),
        (sums, data_vec, noise_var.reshape(1, 64)),
        (whole(),) * 3,
    )


def solution(mesh):
    return jax.shard_map(
        shards,
        mesh=mesh,
        in_specs=(
            P("tm", None, "stripe"),
            P("tm", None, None, "stripe"),
            P("tm"),
            P(),
            P("stripe"),
        ),
        out_specs=P("tm", None, "stripe"),
        check_vma=False,
    )
```

```python
import functools
import math

import jax
import jax.numpy as jnp
import numpy as np
from jax import lax
from jax.experimental import pallas as pl
from jax.experimental.pallas import tpu as pltpu
from jax.sharding import PartitionSpec as P

exact = lax.Precision.HIGHEST
f32 = jnp.float32
bf16 = jnp.bfloat16


def whole():
    return pl.BlockSpec(memory_space=pltpu.VMEM)


def scalars():
    return pl.BlockSpec(memory_space=pltpu.SMEM)


def call(body, out_shape, operands, specs, scratch=(), limit=4 << 20, hint=1e6):
    return pl.pallas_call(
        body,
        out_shape=out_shape,
        in_specs=list(specs),
        out_specs=whole(),
        scratch_shapes=list(scratch),
        cost_estimate=pl.CostEstimate(
            flops=int(hint), transcendentals=0, bytes_accessed=100_000
        ),
        compiler_params=pltpu.CompilerParams(vmem_limit_bytes=limit),
    )(*operands)


def mm(a, b, dims=((1,), (0,)), precision=exact):
    return lax.dot_general(
        a, b, (dims, ((), ())), precision=precision, preferred_element_type=f32
    )


def fourier_table(blocks):
    steps = np.arange(128)
    angles = np.outer(steps, steps) % 256 * (math.pi / 128)
    pair = np.stack([np.cos(angles), -np.sin(angles)]) / math.sqrt(128)
    pair = pair.reshape(2, blocks, 128 // blocks, 128).transpose(1, 0, 2, 3)
    return pair.reshape(blocks, 2 * (128 // blocks), 128).astype(np.float32)


def sine_matrix(length):
    numbers = np.arange(length) + 1
    product = np.outer(numbers, numbers) % (2 * (length + 1))
    return np.sin(product * (math.pi / (length + 1))) * math.sqrt(2.0 / (length + 1))


def row_order():
    stripe, parity, c = np.meshgrid(np.arange(8), np.arange(2), np.arange(8), indexing="ij")
    return (stripe * 16 + 2 * c + parity).reshape(-1)


def low_half(shape):
    return lax.broadcasted_iota(jnp.int32, shape, len(shape) - 1) < 64


def swap_halves(first, second):
    keep = low_half(first.shape)
    low = jnp.where(keep, first, pltpu.roll(second, 64, 1))
    high = jnp.where(keep, pltpu.roll(first, 64, 1), second)
    return low, high


def spread_body(data_ref, out_ref):
    flat = jnp.concatenate([data_ref[:, 0, :], data_ref[:, 1, :]], axis=1)
    two = jnp.concatenate([flat, flat], axis=0)
    for r in range(16):
        out_ref[r * 8 : r * 8 + 8, :] = two


def spectra_body(data_ref, table_ref, out_ref):
    tm = lax.axis_index("tm")
    spectra = mm(table_ref[tm], data_ref[...]).astype(bf16)
    for r in range(8):
        out_ref[r] = spectra


def adjoint_body(gathered_ref, kernel_ref, scale_ref, column_ref, out_ref, grid_ref):
    parts = [[], []]
    for j in range(4):
        first = gathered_ref[2 * j].astype(f32)
        second = gathered_ref[2 * j + 1].astype(f32)
        low, high = swap_halves(first, second)
        parts[0].append(low)
        parts[1].append(high)
    rows = [jnp.concatenate(part, axis=1) for part in parts]
    sub = lax.broadcasted_iota(jnp.int32, (8, 512), 0)
    turned = [jnp.where(sub < 4, pltpu.roll(r, 4, 0), -pltpu.roll(r, 4, 0)) for r in rows]
    straight = jnp.concatenate(rows, axis=0)
    turned = jnp.concatenate(turned, axis=0)
    freq = lax.broadcasted_iota(jnp.int32, (16, 512), 0) % 4
    total = None
    for k in range(4):
        for c, source in enumerate((straight, turned)):
            left = jnp.where(freq == k, source, 0.0).astype(bf16)
            term = mm(left, kernel_ref[k, c], precision=None)
            total = term if total is None else total + term
    row = lax.broadcasted_iota(jnp.int32, (16, 1024), 0) % 4
    scale = jnp.where(
        row < 2,
        jnp.where(row == 0, scale_ref[0], scale_ref[1]),
        jnp.where(row == 2, scale_ref[2], scale_ref[3]),
    )
    total = total * scale
    stack = jnp.concatenate([total[:, c * 128 : c * 128 + 128] for c in range(8)], axis=0)
    grid_ref[...] = mm(stack, column_ref[...])
    for m in range(8):
        first = grid_ref[pl.ds(2 * m, 8, stride=16), :]
        second = grid_ref[pl.ds(2 * m + 1, 8, stride=16), :]
        low, high = swap_halves(first, second)
        for r in range(8):
            out_ref[r, 0:8, m * 128 : m * 128 + 128] = low
            out_ref[r, 8:16, m * 128 : m * 128 + 128] = high


def images_body(
    grids_ref, kernel_ref, prior_ref, forward_ref, backward_ref, column_ref, out_ref, grid_ref
):
    stripe = lax.axis_index("stripe")
    modes = mm(forward_ref[...], grids_ref[...])
    prior = prior_ref[...].T
    prior = jnp.concatenate([prior, prior], axis=1)
    modes = modes * jnp.concatenate([prior] * 8, axis=1)
    back = mm(backward_ref[pl.ds(stripe * 16, 16), :], modes)
    for m in range(8):
        first, second = swap_halves(
            back[0:8, m * 128 : m * 128 + 128], back[8:16, m * 128 : m * 128 + 128]
        )
        grid_ref[pl.ds(2 * m, 8, stride=16), :] = first
        grid_ref[pl.ds(2 * m + 1, 8, stride=16), :] = second
    smooth = mm(grid_ref[...], column_ref[...])
    smooth = jnp.concatenate([smooth[c * 16 : c * 16 + 16, :] for c in range(8)], axis=1)
    sub = lax.broadcasted_iota(jnp.int32, (8, 1024), 0)
    turned = []
    for n in range(2):
        moved = pltpu.roll(smooth[n * 8 : n * 8 + 8, :], 4, 0)
        turned.append(jnp.where(sub < 4, -moved, moved))
    turned = jnp.concatenate(turned, axis=0)
    freq = lax.broadcasted_iota(jnp.int32, (16, 1024), 0) % 4
    total = None
    for k in range(4):
        for c, source in enumerate((smooth, turned)):
            left = jnp.where(freq == k, source, 0.0).astype(bf16)
            term = mm(left, kernel_ref[k, c], ((1,), (1,)), precision=None)
            total = term if total is None else total + term
    for j in range(4):
        low, high = swap_halves(
            total[0:8, j * 128 : j * 128 + 128], total[8:16, j * 128 : j * 128 + 128]
        )
        out_ref[2 * j] = low
        out_ref[2 * j + 1] = high


def times_body(images_ref, table_ref, out_ref):
    tm = lax.axis_index("tm")
    total = images_ref[0]
    for r in range(1, 8):
        total = total + images_ref[r]
    out_ref[...] = mm(table_ref[tm], total, ((0,), (0,)))


def finish_body(sums_ref, data_ref, noise_ref, out_ref):
    total = sums_ref[0:8, :]
    for r in range(1, 16):
        total = total + sums_ref[r * 8 : r * 8 + 8, :]
    total = total[0:4, :] + total[4:8, :]
    noise = noise_ref[...]
    out_ref[:, 0, :] = total[:, 0:64] + noise * data_ref[:, 0, :]
    out_ref[:, 1, :] = total[:, 64:128] + noise * data_ref[:, 1, :]


def exchange(x, axis):
    return lax.all_to_all(x, axis, 0, 0, tiled=True)


def shards(data_vec, kernel, time_spectrum, prior_spectrum, noise_var):
    table = jnp.asarray(fourier_table(32))
    rows = sine_matrix(128)
    order = row_order()
    backward = jnp.asarray(rows[order].astype(np.float32))
    forward = jnp.asarray(rows[:, order].astype(np.float32))
    columns = sine_matrix(64)
    column = jnp.asarray(np.kron(np.eye(2), columns).astype(np.float32))

    spread = call(
        spread_body,
        jax.ShapeDtypeStruct((128, 128), f32),
        (data_vec,),
        (whole(),),
        hint=2e10,
    )
    by_time = exchange(spread.reshape(32, 4, 128), "tm").reshape(128, 128)
    spectra = call(
        spectra_body,
        jax.ShapeDtypeStruct((8, 8, 128), bf16),
        (by_time, table),
        (whole(), whole()),
        hint=2e10,
    )
    gathered = exchange(spectra, "stripe")
    grids = call(
        adjoint_body,
        jax.ShapeDtypeStruct((8, 16, 1024), f32),
        (gathered, kernel, time_spectrum, column),
        (whole(), whole(), scalars(), whole()),
        (pltpu.VMEM((128, 128), f32),),
        limit=20 << 20,
    )
    grids = exchange(grids, "stripe").reshape(128, 1024)
    images = call(
        images_body,
        jax.ShapeDtypeStruct((8, 8, 128), f32),
        (grids, kernel, prior_spectrum.T, forward, backward, column),
        (whole(),) * 6,
        (pltpu.VMEM((128, 128), f32),),
        limit=20 << 20,
    )
    images = exchange(images, "stripe")
    sums = call(
        times_body, jax.ShapeDtypeStruct((128, 128), f32), (images, table), (whole(), whole())
    )
    sums = exchange(sums.reshape(32, 4, 128), "tm").reshape(128, 128)
    return call(
        finish_body,
        jax.ShapeDtypeStruct((4, 2, 64), f32),
        (sums, data_vec, noise_var.reshape(1, 64)),
        (whole(),) * 3,
    )


def solution(mesh):
    return jax.shard_map(
        shards,
        mesh=mesh,
        in_specs=(
            P("tm", None, "stripe"),
            P("tm", None, None, "stripe"),
            P("tm"),
            P(),
            P("stripe"),
        ),
        out_specs=P("tm", None, "stripe"),
        check_vma=False,
    )
```

```python
import functools
import math

import jax
import jax.numpy as jnp
import numpy as np
from jax import lax
from jax.experimental import pallas as pl
from jax.experimental.pallas import tpu as pltpu
from jax.sharding import PartitionSpec as P

exact = lax.Precision.HIGHEST
f32 = jnp.float32
bf16 = jnp.bfloat16


def whole():
    return pl.BlockSpec(memory_space=pltpu.VMEM)


def scalars():
    return pl.BlockSpec(memory_space=pltpu.SMEM)


def call(body, out_shape, operands, specs, scratch=(), limit=4 << 20, hint=1e6):
    return pl.pallas_call(
        body,
        out_shape=out_shape,
        in_specs=list(specs),
        out_specs=whole(),
        scratch_shapes=list(scratch),
        cost_estimate=pl.CostEstimate(
            flops=int(hint), transcendentals=0, bytes_accessed=100_000
        ),
        compiler_params=pltpu.CompilerParams(vmem_limit_bytes=limit),
    )(*operands)


def mm(a, b, dims=((1,), (0,)), precision=exact):
    return lax.dot_general(
        a, b, (dims, ((), ())), precision=precision, preferred_element_type=f32
    )


def fourier_table(halves, blocks):
    steps = np.arange(128)
    angles = np.outer(steps, steps) % 256 * (math.pi / 128)
    pair = np.stack([np.cos(angles), -np.sin(angles)]) / math.sqrt(128)
    pair = pair.reshape(2, halves, blocks, 4, halves, 64).transpose(4, 2, 1, 0, 3, 5)
    return pair.reshape(halves, blocks, halves * 8, 64).astype(np.float32)


def sine_matrix(length):
    numbers = np.arange(length) + 1
    product = np.outer(numbers, numbers) % (2 * (length + 1))
    return np.sin(product * (math.pi / (length + 1))) * math.sqrt(2.0 / (length + 1))


def row_order():
    stripe, parity, c = np.meshgrid(np.arange(8), np.arange(2), np.arange(8), indexing="ij")
    return (stripe * 16 + 2 * c + parity).reshape(-1)


def low_half(shape):
    return lax.broadcasted_iota(jnp.int32, shape, len(shape) - 1) < 64


def swap_halves(first, second):
    keep = low_half(first.shape)
    low = jnp.where(keep, first, pltpu.roll(second, 64, 1))
    high = jnp.where(keep, pltpu.roll(first, 64, 1), second)
    return low, high


def split(x):
    high = x.astype(bf16)
    return high, (x - high.astype(f32)).astype(bf16)


def split_table(x):
    high = x.astype(np.float32).astype(bf16)
    return high, (x - high.astype(np.float64)).astype(np.float32).astype(bf16)


def column_transform(x, high_ref, low_ref):
    high, low = split(x)
    return (
        mm(high, high_ref[...], precision=None)
        + mm(low, high_ref[...], precision=None)
        + mm(high, low_ref[...], precision=None)
    )


def spread_body(data_ref, out_ref):
    flat = jnp.concatenate([data_ref[:, 0, :], data_ref[:, 1, :]], axis=1)
    two = jnp.concatenate([flat, flat], axis=0)
    for r in range(8):
        out_ref[r * 8 : r * 8 + 8, :] = two


def block_of_table(table_ref):
    tm = lax.axis_index("tm")
    return table_ref[tm // 16, tm % 16]


def spectra_body(data_ref, table_ref, out_ref):
    spectra = mm(block_of_table(table_ref), data_ref[...])
    for half in range(2):
        for r in range(8):
            out_ref[half, r] = spectra[half * 8 : half * 8 + 8, :]


def adjoint_body(gathered_ref, kernel_ref, scale_ref, high_ref, low_ref, out_ref, grid_ref):
    parts = [[], []]
    for j in range(4):
        first = gathered_ref[0, 2 * j] + gathered_ref[1, 2 * j]
        second = gathered_ref[0, 2 * j + 1] + gathered_ref[1, 2 * j + 1]
        low, high = swap_halves(first, second)
        parts[0].append(low)
        parts[1].append(high)
    rows = [jnp.concatenate(part, axis=1) for part in parts]
    sub = lax.broadcasted_iota(jnp.int32, (8, 512), 0)
    turned = [jnp.where(sub < 4, pltpu.roll(r, 4, 0), -pltpu.roll(r, 4, 0)) for r in rows]
    straight = jnp.concatenate(rows, axis=0)
    turned = jnp.concatenate(turned, axis=0)
    freq = lax.broadcasted_iota(jnp.int32, (16, 512), 0) % 4
    total = None
    for k in range(4):
        for c, source in enumerate((straight, turned)):
            left = jnp.where(freq == k, source, 0.0).astype(bf16)
            term = mm(left, kernel_ref[k, c], precision=None)
            total = term if total is None else total + term
    row = lax.broadcasted_iota(jnp.int32, (16, 1024), 0) % 4
    scale = jnp.where(
        row < 2,
        jnp.where(row == 0, scale_ref[0], scale_ref[1]),
        jnp.where(row == 2, scale_ref[2], scale_ref[3]),
    )
    total = total * scale
    stack = jnp.concatenate([total[:, c * 128 : c * 128 + 128] for c in range(8)], axis=0)
    grid_ref[...] = column_transform(stack, high_ref, low_ref)
    for m in range(8):
        first = grid_ref[pl.ds(2 * m, 8, stride=16), :]
        second = grid_ref[pl.ds(2 * m + 1, 8, stride=16), :]
        tile = jnp.concatenate(swap_halves(first, second), axis=0).astype(bf16)
        for r in range(8):
            out_ref[r, :, m * 128 : m * 128 + 128] = tile


def images_body(
    grids_ref, kernel_ref, prior_ref, forward_ref, backward_ref, high_ref, low_ref, out_ref, grid_ref
):
    stripe = lax.axis_index("stripe")
    grids = grids_ref[...]
    modes = mm(forward_ref[...], jnp.concatenate([grids, grids], axis=0), precision=None)
    prior = prior_ref[...].T
    prior = jnp.concatenate([prior, prior], axis=1)
    modes = modes * jnp.concatenate([prior] * 8, axis=1)
    modes = jnp.concatenate(split(modes), axis=0)
    back = mm(backward_ref[stripe], modes, precision=None)
    back = back[0:16, :] + back[16:32, :]
    for m in range(8):
        first, second = swap_halves(
            back[0:8, m * 128 : m * 128 + 128], back[8:16, m * 128 : m * 128 + 128]
        )
        grid_ref[pl.ds(2 * m, 8, stride=16), :] = first
        grid_ref[pl.ds(2 * m + 1, 8, stride=16), :] = second
    smooth = column_transform(grid_ref[...], high_ref, low_ref)
    smooth = jnp.concatenate([smooth[c * 16 : c * 16 + 16, :] for c in range(8)], axis=1)
    sub = lax.broadcasted_iota(jnp.int32, (8, 1024), 0)
    turned = []
    for n in range(2):
        moved = pltpu.roll(smooth[n * 8 : n * 8 + 8, :], 4, 0)
        turned.append(jnp.where(sub < 4, -moved, moved))
    turned = jnp.concatenate(turned, axis=0)
    freq = lax.broadcasted_iota(jnp.int32, (16, 1024), 0) % 4
    total = None
    for k in range(4):
        for c, source in enumerate((smooth, turned)):
            left = jnp.where(freq == k, source, 0.0).astype(bf16)
            term = mm(left, kernel_ref[k, c], ((1,), (1,)), precision=None)
            total = term if total is None else total + term
    for j in range(4):
        low, high = swap_halves(
            total[0:8, j * 128 : j * 128 + 128], total[8:16, j * 128 : j * 128 + 128]
        )
        for half in range(2):
            out_ref[half, 2 * j] = low
            out_ref[half, 2 * j + 1] = high


def times_body(images_ref, table_ref, out_ref):
    halves = []
    for half in range(2):
        total = images_ref[half, 0]
        for r in range(1, 8):
            total = total + images_ref[half, r]
        halves.append(total)
    images = jnp.concatenate(halves, axis=0)
    out_ref[...] = mm(block_of_table(table_ref), images, ((0,), (0,)))


def finish_body(sums_ref, data_ref, noise_ref, out_ref):
    total = sums_ref[0:8, :]
    for r in range(1, 8):
        total = total + sums_ref[r * 8 : r * 8 + 8, :]
    total = total[0:4, :] + total[4:8, :]
    noise = noise_ref[...]
    out_ref[:, 0, :] = total[:, 0:64] + noise * data_ref[:, 0, :]
    out_ref[:, 1, :] = total[:, 64:128] + noise * data_ref[:, 1, :]


def exchange(x, axis, groups=None):
    return lax.all_to_all(x, axis, 0, 0, tiled=True, axis_index_groups=groups)


def shards(data_vec, kernel, time_spectrum, prior_spectrum, noise_var):
    table = jnp.asarray(fourier_table(2, 16))
    rows = sine_matrix(128)
    order = row_order()
    forward = jnp.asarray(np.concatenate(split_table(rows[:, order]), axis=1))
    high, low = split_table(rows[order].reshape(8, 16, 128))
    upper = np.concatenate([high, high], axis=2)
    lower = np.concatenate([low, np.zeros_like(low)], axis=2)
    backward = jnp.asarray(np.concatenate([upper, lower], axis=1))
    columns = [jnp.asarray(t) for t in split_table(np.kron(np.eye(2), sine_matrix(64)))]

    first = [[half * 16 + block for block in range(16)] for half in range(2)]
    second = [
        [(half * 16 + block) * 8 + stripe for half in range(2) for stripe in range(8)]
        for block in range(16)
    ]

    spread = call(
        spread_body,
        jax.ShapeDtypeStruct((64, 128), f32),
        (data_vec,),
        (whole(),),
        hint=2e10,
    )
    by_time = exchange(spread.reshape(16, 4, 128), "tm", first).reshape(64, 128)
    spectra = call(
        spectra_body,
        jax.ShapeDtypeStruct((2, 8, 8, 128), f32),
        (by_time, table),
        (whole(), whole()),
        hint=2e10,
    )
    gathered = exchange(spectra.reshape(16, 8, 128), ("tm", "stripe"), second)
    grids = call(
        adjoint_body,
        jax.ShapeDtypeStruct((8, 16, 1024), bf16),
        (gathered.reshape(2, 8, 8, 128), kernel, time_spectrum, *columns),
        (whole(), whole(), scalars(), whole(), whole()),
        (pltpu.VMEM((128, 128), f32),),
        limit=20 << 20,
    )
    grids = exchange(grids, "stripe").reshape(128, 1024)
    images = call(
        images_body,
        jax.ShapeDtypeStruct((2, 8, 8, 128), f32),
        (grids, kernel, prior_spectrum.T, forward, backward, *columns),
        (whole(),) * 7,
        (pltpu.VMEM((128, 128), f32),),
        limit=20 << 20,
    )
    images = exchange(images.reshape(16, 8, 128), ("tm", "stripe"), second)
    sums = call(
        times_body,
        jax.ShapeDtypeStruct((64, 128), f32),
        (images.reshape(2, 8, 8, 128), table),
        (whole(), whole()),
    )
    sums = exchange(sums.reshape(16, 4, 128), "tm", first).reshape(64, 128)
    return call(
        finish_body,
        jax.ShapeDtypeStruct((4, 2, 64), f32),
        (sums, data_vec, noise_var.reshape(1, 64)),
        (whole(),) * 3,
    )


def solution(mesh):
    return jax.shard_map(
        shards,
        mesh=mesh,
        in_specs=(
            P("tm", None, "stripe"),
            P("tm", None, None, "stripe"),
            P("tm"),
            P(),
            P("stripe"),
        ),
        out_specs=P("tm", None, "stripe"),
        check_vma=False,
    )
```

```python
import functools
import math

import jax
import jax.numpy as jnp
import numpy as np
from jax import lax
from jax.experimental import pallas as pl
from jax.experimental.pallas import tpu as pltpu
from jax.sharding import PartitionSpec as P

exact = lax.Precision.HIGHEST
f32 = jnp.float32
bf16 = jnp.bfloat16


def whole():
    return pl.BlockSpec(memory_space=pltpu.VMEM)


def scalars():
    return pl.BlockSpec(memory_space=pltpu.SMEM)


def call(body, out_shape, operands, specs, scratch=(), limit=4 << 20, hint=1e6):
    return pl.pallas_call(
        body,
        out_shape=out_shape,
        in_specs=list(specs),
        out_specs=whole(),
        scratch_shapes=list(scratch),
        cost_estimate=pl.CostEstimate(
            flops=int(hint), transcendentals=0, bytes_accessed=100_000
        ),
        compiler_params=pltpu.CompilerParams(vmem_limit_bytes=limit),
    )(*operands)


def mm(a, b, dims=((1,), (0,)), precision=exact):
    return lax.dot_general(
        a, b, (dims, ((), ())), precision=precision, preferred_element_type=f32
    )


def fourier_table(halves, blocks):
    steps = np.arange(128)
    angles = np.outer(steps, steps) % 256 * (math.pi / 128)
    pair = np.stack([np.cos(angles), -np.sin(angles)]) / math.sqrt(128)
    pair = pair.reshape(2, halves, blocks, 4, halves, 64).transpose(4, 2, 1, 0, 3, 5)
    return pair.reshape(halves, blocks, halves * 8, 64).astype(np.float32)


def inverse_table():
    steps = np.arange(128)
    angles = np.outer(steps, steps) % 256 * (math.pi / 128)
    pair = np.stack([np.cos(angles), -np.sin(angles)]) / math.sqrt(128)
    pair = pair.reshape(2, 2, 8, 2, 4, 2, 8, 2, 4)
    pair = pair.transpose(2, 5, 7, 1, 3, 0, 4, 6, 8)
    return pair.reshape(8, 4, 32, 32).astype(np.float32)


def sine_matrix(length):
    numbers = np.arange(length) + 1
    product = np.outer(numbers, numbers) % (2 * (length + 1))
    return np.sin(product * (math.pi / (length + 1))) * math.sqrt(2.0 / (length + 1))


def row_order():
    stripe, parity, c = np.meshgrid(np.arange(8), np.arange(2), np.arange(8), indexing="ij")
    return (stripe * 16 + 2 * c + parity).reshape(-1)


def low_half(shape):
    return lax.broadcasted_iota(jnp.int32, shape, len(shape) - 1) < 64


def swap_halves(first, second):
    keep = low_half(first.shape)
    low = jnp.where(keep, first, pltpu.roll(second, 64, 1))
    high = jnp.where(keep, pltpu.roll(first, 64, 1), second)
    return low, high


def split(x):
    high = x.astype(bf16)
    return high, (x - high.astype(f32)).astype(bf16)


def split_table(x):
    high = x.astype(np.float32).astype(bf16)
    return high, (x - high.astype(np.float64)).astype(np.float32).astype(bf16)


def column_transform(x, high_ref, low_ref):
    high, low = split(x)
    return (
        mm(high, high_ref[...], precision=None)
        + mm(low, high_ref[...], precision=None)
        + mm(high, low_ref[...], precision=None)
    )


def spread_body(data_ref, out_ref):
    flat = jnp.concatenate([data_ref[:, 0, :], data_ref[:, 1, :]], axis=1)
    two = jnp.concatenate([flat, flat], axis=0)
    for r in range(8):
        out_ref[r * 8 : r * 8 + 8, :] = two


def block_of_table(table_ref):
    tm = lax.axis_index("tm")
    return table_ref[tm // 16, tm % 16]


def spectra_body(data_ref, table_ref, out_ref):
    spectra = mm(block_of_table(table_ref), data_ref[...])
    for half in range(2):
        for r in range(8):
            out_ref[half, r] = spectra[half * 8 : half * 8 + 8, :]


def adjoint_body(gathered_ref, kernel_ref, scale_ref, high_ref, low_ref, out_ref, grid_ref):
    parts = [[], []]
    for j in range(4):
        first = gathered_ref[0, 2 * j] + gathered_ref[1, 2 * j]
        second = gathered_ref[0, 2 * j + 1] + gathered_ref[1, 2 * j + 1]
        low, high = swap_halves(first, second)
        parts[0].append(low)
        parts[1].append(high)
    rows = [jnp.concatenate(part, axis=1) for part in parts]
    sub = lax.broadcasted_iota(jnp.int32, (8, 512), 0)
    turned = [jnp.where(sub < 4, pltpu.roll(r, 4, 0), -pltpu.roll(r, 4, 0)) for r in rows]
    straight = jnp.concatenate(rows, axis=0)
    turned = jnp.concatenate(turned, axis=0)
    both = jnp.concatenate([straight, turned], axis=1)
    freq = lax.broadcasted_iota(jnp.int32, (16, 1024), 0) % 4
    total = None
    for k in range(4):
        left = jnp.where(freq == k, both, 0.0).astype(bf16)
        term = mm(left, kernel_ref[k].reshape(1024, 1024), precision=None)
        total = term if total is None else total + term
    row = lax.broadcasted_iota(jnp.int32, (16, 1024), 0) % 4
    scale = jnp.where(
        row < 2,
        jnp.where(row == 0, scale_ref[0], scale_ref[1]),
        jnp.where(row == 2, scale_ref[2], scale_ref[3]),
    )
    total = total * scale
    stack = jnp.concatenate([total[:, c * 128 : c * 128 + 128] for c in range(8)], axis=0)
    grid_ref[...] = column_transform(stack, high_ref, low_ref)
    for m in range(8):
        first = grid_ref[pl.ds(2 * m, 8, stride=16), :]
        second = grid_ref[pl.ds(2 * m + 1, 8, stride=16), :]
        tile = jnp.concatenate(swap_halves(first, second), axis=0).astype(bf16)
        for r in range(8):
            out_ref[r, :, m * 128 : m * 128 + 128] = tile


def images_body(
    grids_ref, kernel_ref, prior_ref, forward_ref, backward_ref, high_ref, low_ref, out_ref, grid_ref
):
    stripe = lax.axis_index("stripe")
    grids = grids_ref[...]
    modes = mm(forward_ref[...], jnp.concatenate([grids, grids], axis=0), precision=None)
    prior = prior_ref[...].T
    prior = jnp.concatenate([prior, prior], axis=1)
    modes = modes * jnp.concatenate([prior] * 8, axis=1)
    modes = jnp.concatenate(split(modes), axis=0)
    back = mm(backward_ref[stripe], modes, precision=None)
    back = back[0:16, :] + back[16:32, :]
    for m in range(8):
        first, second = swap_halves(
            back[0:8, m * 128 : m * 128 + 128], back[8:16, m * 128 : m * 128 + 128]
        )
        grid_ref[pl.ds(2 * m, 8, stride=16), :] = first
        grid_ref[pl.ds(2 * m + 1, 8, stride=16), :] = second
    smooth = column_transform(grid_ref[...], high_ref, low_ref)
    smooth = jnp.concatenate([smooth[c * 16 : c * 16 + 16, :] for c in range(8)], axis=1)
    left = smooth.astype(bf16)
    products = mm(left, kernel_ref[...].reshape(4096, 1024), ((1,), (1,)), precision=None)
    freq = lax.broadcasted_iota(jnp.int32, (16, 1024), 0) % 4
    total = jnp.where(freq == 0, products[:, 0:1024], 0.0)
    for k in range(1, 4):
        total = jnp.where(freq == k, products[:, k * 1024 : k * 1024 + 1024], total)
    sub = lax.broadcasted_iota(jnp.int32, (8, 512), 0)
    rows = []
    for n in range(2):
        moved = pltpu.roll(total[n * 8 : n * 8 + 8, 512:], 4, 0)
        rows.append(total[n * 8 : n * 8 + 8, :512] + jnp.where(sub < 4, -moved, moved))
    total = jnp.concatenate(rows, axis=0)
    for j in range(4):
        low, high = swap_halves(
            total[0:8, j * 128 : j * 128 + 128], total[8:16, j * 128 : j * 128 + 128]
        )
        low, high = low.astype(bf16), high.astype(bf16)
        for copy in range(4):
            out_ref[copy, 2 * j] = low
            out_ref[copy, 2 * j + 1] = high


def times_body(images_ref, table_ref, out_ref):
    tm = lax.axis_index("tm")
    blocks = []
    for block in range(4):
        total = images_ref[block, 0].astype(f32)
        for r in range(1, 8):
            total = total + images_ref[block, r].astype(f32)
        blocks.append(total)
    images = jnp.concatenate(blocks, axis=0)
    table = table_ref[tm % 16 // 2, tm // 16 * 2 + tm % 2]
    out_ref[...] = mm(table, images, ((0,), (0,)))


def finish_body(sums_ref, data_ref, noise_ref, out_ref):
    total = sums_ref[0:8, :]
    for r in range(1, 4):
        total = total + sums_ref[r * 8 : r * 8 + 8, :]
    total = total[0:4, :] + total[4:8, :]
    noise = noise_ref[...]
    out_ref[:, 0, :] = total[:, 0:64] + noise * data_ref[:, 0, :]
    out_ref[:, 1, :] = total[:, 64:128] + noise * data_ref[:, 1, :]


def exchange(x, axis, groups=None):
    return lax.all_to_all(x, axis, 0, 0, tiled=True, axis_index_groups=groups)


def shards(data_vec, kernel, time_spectrum, prior_spectrum, noise_var):
    table = jnp.asarray(fourier_table(2, 16))
    rows = sine_matrix(128)
    order = row_order()
    forward = jnp.asarray(np.concatenate(split_table(rows[:, order]), axis=1))
    high, low = split_table(rows[order].reshape(8, 16, 128))
    upper = np.concatenate([high, high], axis=2)
    lower = np.concatenate([low, np.zeros_like(low)], axis=2)
    backward = jnp.asarray(np.concatenate([upper, lower], axis=1))
    columns = [jnp.asarray(t) for t in split_table(np.kron(np.eye(2), sine_matrix(64)))]

    first = [[half * 16 + block for block in range(16)] for half in range(2)]
    second = [
        [(half * 16 + block) * 8 + stripe for half in range(2) for stripe in range(8)]
        for block in range(16)
    ]

    third = [
        [
            (half * 16 + z * 2 + core) * 8 + stripe
            for half in range(2)
            for core in range(2)
            for stripe in range(8)
        ]
        for z in range(8)
    ]
    fourth = [
        [half * 16 + z * 2 + core for z in range(8)] for half in range(2) for core in range(2)
    ]

    spread = call(
        spread_body,
        jax.ShapeDtypeStruct((64, 128), f32),
        (data_vec,),
        (whole(),),
        hint=2e10,
    )
    by_time = exchange(spread.reshape(16, 4, 128), "tm", first).reshape(64, 128)
    spectra = call(
        spectra_body,
        jax.ShapeDtypeStruct((2, 8, 8, 128), f32),
        (by_time, table),
        (whole(), whole()),
        hint=2e10,
    )
    gathered = exchange(spectra.reshape(16, 8, 128), ("tm", "stripe"), second)
    grids = call(
        adjoint_body,
        jax.ShapeDtypeStruct((8, 16, 1024), bf16),
        (gathered.reshape(2, 8, 8, 128), kernel, time_spectrum, *columns),
        (whole(), whole(), scalars(), whole(), whole()),
        (pltpu.VMEM((128, 128), f32),),
        limit=20 << 20,
    )
    grids = exchange(grids, "stripe").reshape(128, 1024)
    images = call(
        images_body,
        jax.ShapeDtypeStruct((4, 8, 8, 128), bf16),
        (grids, kernel, prior_spectrum.T, forward, backward, *columns),
        (whole(),) * 7,
        (pltpu.VMEM((128, 128), f32),),
        limit=20 << 20,
    )
    images = exchange(images.reshape(32, 8, 128), ("tm", "stripe"), third)
    sums = call(
        times_body,
        jax.ShapeDtypeStruct((32, 128), f32),
        (images.reshape(4, 8, 8, 128), jnp.asarray(inverse_table())),
        (whole(), whole()),
    )
    sums = exchange(sums.reshape(8, 4, 128), "tm", fourth).reshape(32, 128)
    return call(
        finish_body,
        jax.ShapeDtypeStruct((4, 2, 64), f32),
        (sums, data_vec, noise_var.reshape(1, 64)),
        (whole(),) * 3,
    )


def solution(mesh):
    return jax.shard_map(
        shards,
        mesh=mesh,
        in_specs=(
            P("tm", None, "stripe"),
            P("tm", None, None, "stripe"),
            P("tm"),
            P(),
            P("stripe"),
        ),
        out_specs=P("tm", None, "stripe"),
        check_vma=False,
    )
```

```python
import math

import jax
import jax.numpy as jnp
import numpy as np
from jax import lax
from jax.experimental import pallas as pl
from jax.experimental.pallas import tpu as pltpu
from jax.sharding import Mesh
from jax.sharding import PartitionSpec as P

exact = lax.Precision.HIGHEST
f32 = jnp.float32
bf16 = jnp.bfloat16


def whole():
    return pl.BlockSpec(memory_space=pltpu.VMEM)


def scalars():
    return pl.BlockSpec(memory_space=pltpu.SMEM)


def call(body, out_shape, operands, specs, scratch=(), limit=4 << 20, hint=1e6):
    return pl.pallas_call(
        body,
        out_shape=out_shape,
        in_specs=list(specs),
        out_specs=whole(),
        scratch_shapes=list(scratch),
        cost_estimate=pl.CostEstimate(
            flops=int(hint), transcendentals=0, bytes_accessed=100_000
        ),
        compiler_params=pltpu.CompilerParams(vmem_limit_bytes=limit),
    )(*operands)


def mm(a, b, dims=((1,), (0,)), precision=exact):
    return lax.dot_general(
        a, b, (dims, ((), ())), precision=precision, preferred_element_type=f32
    )


def fourier_table(halves, blocks):
    steps = np.arange(128)
    angles = np.outer(steps, steps) % 256 * (math.pi / 128)
    pair = np.stack([np.cos(angles), -np.sin(angles)]) / math.sqrt(128)
    pair = pair.reshape(2, halves, blocks, 4, halves, 64).transpose(4, 2, 1, 0, 3, 5)
    return pair.reshape(halves, blocks, halves * 8, 64).astype(np.float32)


def inverse_table():
    steps = np.arange(128)
    angles = np.outer(steps, steps) % 256 * (math.pi / 128)
    pair = np.stack([np.cos(angles), -np.sin(angles)]) / math.sqrt(128)
    pair = pair.reshape(2, 2, 8, 2, 4, 2, 8, 2, 4)
    pair = pair.transpose(2, 5, 7, 1, 3, 0, 4, 6, 8)
    return pair.reshape(8, 4, 32, 32).astype(np.float32)


def sine_matrix(length):
    numbers = np.arange(length) + 1
    product = np.outer(numbers, numbers) % (2 * (length + 1))
    return np.sin(product * (math.pi / (length + 1))) * math.sqrt(2.0 / (length + 1))


def row_order():
    stripe, parity, c = np.meshgrid(np.arange(8), np.arange(2), np.arange(8), indexing="ij")
    return (stripe * 16 + 2 * c + parity).reshape(-1)


def low_half(shape):
    return lax.broadcasted_iota(jnp.int32, shape, len(shape) - 1) < 64


def swap_halves(first, second):
    keep = low_half(first.shape)
    low = jnp.where(keep, first, pltpu.roll(second, 64, 1))
    high = jnp.where(keep, pltpu.roll(first, 64, 1), second)
    return low, high


def split(x):
    high = x.astype(bf16)
    return high, (x - high.astype(f32)).astype(bf16)


def split_table(x):
    high = x.astype(np.float32).astype(bf16)
    return high, (x - high.astype(np.float64)).astype(np.float32).astype(bf16)


def column_transform(x, high_ref, low_ref):
    high, low = split(x)
    return (
        mm(high, high_ref[...], precision=None)
        + mm(low, high_ref[...], precision=None)
        + mm(high, low_ref[...], precision=None)
    )


def spread_body(data_ref, out_ref):
    flat = jnp.concatenate([data_ref[:, 0, :], data_ref[:, 1, :]], axis=1)
    two = jnp.concatenate([flat, flat], axis=0)
    for r in range(8):
        out_ref[r * 8 : r * 8 + 8, :] = two


def block_of_table(table_ref):
    return table_ref[lax.axis_index("x_hi"), lax.axis_index("z") * 2 + lax.axis_index("core")]


def spectra_body(data_ref, table_ref, out_ref):
    spectra = mm(block_of_table(table_ref), data_ref[...])
    for half in range(2):
        for r in range(8):
            out_ref[half, r] = spectra[half * 8 : half * 8 + 8, :]


def adjoint_body(gathered_ref, kernel_ref, scale_ref, high_ref, low_ref, out_ref, grid_ref):
    parts = [[], []]
    for j in range(4):
        first = gathered_ref[0, 2 * j] + gathered_ref[1, 2 * j]
        second = gathered_ref[0, 2 * j + 1] + gathered_ref[1, 2 * j + 1]
        low, high = swap_halves(first, second)
        parts[0].append(low)
        parts[1].append(high)
    rows = [jnp.concatenate(part, axis=1) for part in parts]
    sub = lax.broadcasted_iota(jnp.int32, (8, 512), 0)
    turned = [jnp.where(sub < 4, pltpu.roll(r, 4, 0), -pltpu.roll(r, 4, 0)) for r in rows]
    straight = jnp.concatenate(rows, axis=0)
    turned = jnp.concatenate(turned, axis=0)
    both = jnp.concatenate([straight, turned], axis=1)
    freq = lax.broadcasted_iota(jnp.int32, (16, 1024), 0) % 4
    total = None
    for k in range(4):
        left = jnp.where(freq == k, both, 0.0).astype(bf16)
        term = mm(left, kernel_ref[k].reshape(1024, 1024), precision=None)
        total = term if total is None else total + term
    row = lax.broadcasted_iota(jnp.int32, (16, 1024), 0) % 4
    scale = jnp.where(
        row < 2,
        jnp.where(row == 0, scale_ref[0], scale_ref[1]),
        jnp.where(row == 2, scale_ref[2], scale_ref[3]),
    )
    total = total * scale
    stack = jnp.concatenate([total[:, c * 128 : c * 128 + 128] for c in range(8)], axis=0)
    grid_ref[...] = column_transform(stack, high_ref, low_ref)
    for m in range(8):
        first = grid_ref[pl.ds(2 * m, 8, stride=16), :]
        second = grid_ref[pl.ds(2 * m + 1, 8, stride=16), :]
        tile = jnp.concatenate(swap_halves(first, second), axis=0).astype(bf16)
        for r in range(8):
            out_ref[r, :, m * 128 : m * 128 + 128] = tile


def images_body(
    grids_ref, kernel_ref, prior_ref, forward_ref, backward_ref, high_ref, low_ref, out_ref, grid_ref
):
    stripe = lax.axis_index("stripe")
    grids = grids_ref[...]
    modes = mm(forward_ref[...], jnp.concatenate([grids, grids], axis=0), precision=None)
    prior = prior_ref[...].T
    prior = jnp.concatenate([prior, prior], axis=1)
    modes = modes * jnp.concatenate([prior] * 8, axis=1)
    modes = jnp.concatenate(split(modes), axis=0)
    back = mm(backward_ref[stripe], modes, precision=None)
    back = back[0:16, :] + back[16:32, :]
    for m in range(8):
        first, second = swap_halves(
            back[0:8, m * 128 : m * 128 + 128], back[8:16, m * 128 : m * 128 + 128]
        )
        grid_ref[pl.ds(2 * m, 8, stride=16), :] = first
        grid_ref[pl.ds(2 * m + 1, 8, stride=16), :] = second
    smooth = column_transform(grid_ref[...], high_ref, low_ref)
    smooth = jnp.concatenate([smooth[c * 16 : c * 16 + 16, :] for c in range(8)], axis=1)
    left = smooth.astype(bf16)
    products = mm(left, kernel_ref[...].reshape(4096, 1024), ((1,), (1,)), precision=None)
    freq = lax.broadcasted_iota(jnp.int32, (16, 1024), 0) % 4
    total = jnp.where(freq == 0, products[:, 0:1024], 0.0)
    for k in range(1, 4):
        total = jnp.where(freq == k, products[:, k * 1024 : k * 1024 + 1024], total)
    sub = lax.broadcasted_iota(jnp.int32, (8, 512), 0)
    rows = []
    for n in range(2):
        moved = pltpu.roll(total[n * 8 : n * 8 + 8, 512:], 4, 0)
        rows.append(total[n * 8 : n * 8 + 8, :512] + jnp.where(sub < 4, -moved, moved))
    total = jnp.concatenate(rows, axis=0)
    for j in range(4):
        low, high = swap_halves(
            total[0:8, j * 128 : j * 128 + 128], total[8:16, j * 128 : j * 128 + 128]
        )
        low, high = low.astype(bf16), high.astype(bf16)
        for copy in range(4):
            out_ref[copy, 2 * j] = low
            out_ref[copy, 2 * j + 1] = high


def times_body(images_ref, table_ref, out_ref):
    half = lax.axis_index("x_hi") * 2 + lax.axis_index("core")
    blocks = []
    for block in range(4):
        total = images_ref[block, 0].astype(f32)
        for r in range(1, 8):
            total = total + images_ref[block, r].astype(f32)
        blocks.append(total)
    images = jnp.concatenate(blocks, axis=0)
    table = table_ref[lax.axis_index("z"), half]
    out_ref[...] = mm(table, images, ((0,), (0,)))


def finish_body(sums_ref, data_ref, noise_ref, out_ref):
    total = sums_ref[0:8, :]
    for r in range(1, 4):
        total = total + sums_ref[r * 8 : r * 8 + 8, :]
    total = total[0:4, :] + total[4:8, :]
    noise = noise_ref[...]
    out_ref[:, 0, :] = total[:, 0:64] + noise * data_ref[:, 0, :]
    out_ref[:, 1, :] = total[:, 64:128] + noise * data_ref[:, 1, :]


def exchange(x, axes):
    return lax.all_to_all(x, axes, 0, 0, tiled=True)


def shards(data_vec, kernel, time_spectrum, prior_spectrum, noise_var):
    table = jnp.asarray(fourier_table(2, 16))
    rows = sine_matrix(128)
    order = row_order()
    forward = jnp.asarray(np.concatenate(split_table(rows[:, order]), axis=1))
    high, low = split_table(rows[order].reshape(8, 16, 128))
    upper = np.concatenate([high, high], axis=2)
    lower = np.concatenate([low, np.zeros_like(low)], axis=2)
    backward = jnp.asarray(np.concatenate([upper, lower], axis=1))
    columns = [jnp.asarray(t) for t in split_table(np.kron(np.eye(2), sine_matrix(64)))]

    spread = call(
        spread_body,
        jax.ShapeDtypeStruct((64, 128), f32),
        (data_vec,),
        (whole(),),
        hint=2e10,
    )
    by_time = exchange(spread.reshape(16, 4, 128), ("z", "core")).reshape(64, 128)
    spectra = call(
        spectra_body,
        jax.ShapeDtypeStruct((2, 8, 8, 128), f32),
        (by_time, table),
        (whole(), whole()),
        hint=2e10,
    )
    gathered = exchange(spectra.reshape(16, 8, 128), ("x_hi", "stripe"))
    grids = call(
        adjoint_body,
        jax.ShapeDtypeStruct((8, 16, 1024), bf16),
        (gathered.reshape(2, 8, 8, 128), kernel, time_spectrum, *columns),
        (whole(), whole(), scalars(), whole(), whole()),
        (pltpu.VMEM((128, 128), f32),),
        limit=20 << 20,
    )
    grids = exchange(grids, "stripe").reshape(128, 1024)
    images = call(
        images_body,
        jax.ShapeDtypeStruct((4, 8, 8, 128), bf16),
        (grids, kernel, prior_spectrum.T, forward, backward, *columns),
        (whole(),) * 7,
        (pltpu.VMEM((128, 128), f32),),
        limit=20 << 20,
    )
    images = exchange(images.reshape(32, 8, 128), ("x_hi", "core", "stripe"))
    sums = call(
        times_body,
        jax.ShapeDtypeStruct((32, 128), f32),
        (images.reshape(4, 8, 8, 128), jnp.asarray(inverse_table())),
        (whole(), whole()),
    )
    sums = exchange(sums.reshape(8, 4, 128), "z").reshape(32, 128)
    return call(
        finish_body,
        jax.ShapeDtypeStruct((4, 2, 64), f32),
        (sums, data_vec, noise_var.reshape(1, 64)),
        (whole(),) * 3,
    )


def solution(mesh):
    fine = Mesh(mesh.devices.reshape(2, 8, 2, 8), ("x_hi", "z", "core", "stripe"))
    tm = ("x_hi", "z", "core")
    return jax.shard_map(
        shards,
        mesh=fine,
        in_specs=(
            P(tm, None, "stripe"),
            P(tm, None, None, "stripe"),
            P(tm),
            P(),
            P("stripe"),
        ),
        out_specs=P(tm, None, "stripe"),
        check_vma=False,
    )
```

```python
import math

import jax
import jax.numpy as jnp
import numpy as np
from jax import lax
from jax.experimental import pallas as pl
from jax.experimental.pallas import tpu as pltpu
from jax.sharding import Mesh
from jax.sharding import PartitionSpec as P

exact = lax.Precision.HIGHEST
f32 = jnp.float32
bf16 = jnp.bfloat16


def whole():
    return pl.BlockSpec(memory_space=pltpu.VMEM)


def scalars():
    return pl.BlockSpec(memory_space=pltpu.SMEM)


def call(body, out_shape, operands, specs, scratch=(), limit=4 << 20, hint=1e6):
    return pl.pallas_call(
        body,
        out_shape=out_shape,
        in_specs=list(specs),
        out_specs=whole(),
        scratch_shapes=list(scratch),
        cost_estimate=pl.CostEstimate(
            flops=int(hint), transcendentals=0, bytes_accessed=100_000
        ),
        compiler_params=pltpu.CompilerParams(vmem_limit_bytes=limit),
    )(*operands)


def mm(a, b, dims=((1,), (0,)), precision=exact):
    return lax.dot_general(
        a, b, (dims, ((), ())), precision=precision, preferred_element_type=f32
    )


def fourier_table(halves, blocks):
    steps = np.arange(128)
    angles = np.outer(steps, steps) % 256 * (math.pi / 128)
    pair = np.stack([np.cos(angles), -np.sin(angles)]) / math.sqrt(128)
    pair = pair.reshape(2, halves, blocks, 4, halves, 64).transpose(4, 2, 1, 0, 3, 5)
    return pair.reshape(halves, blocks, halves * 8, 64).astype(np.float32)


def inverse_table():
    steps = np.arange(128)
    angles = np.outer(steps, steps) % 256 * (math.pi / 128)
    pair = np.stack([np.cos(angles), -np.sin(angles)]) / math.sqrt(128)
    pair = pair.reshape(2, 2, 8, 2, 4, 2, 8, 2, 4)
    pair = pair.transpose(2, 5, 7, 1, 3, 0, 4, 6, 8)
    return pair.reshape(8, 4, 32, 32).astype(np.float32)


def sine_matrix(length):
    numbers = np.arange(length) + 1
    product = np.outer(numbers, numbers) % (2 * (length + 1))
    return np.sin(product * (math.pi / (length + 1))) * math.sqrt(2.0 / (length + 1))


def row_order():
    stripe, parity, c = np.meshgrid(np.arange(8), np.arange(2), np.arange(8), indexing="ij")
    return (stripe * 16 + 2 * c + parity).reshape(-1)


def low_half(shape):
    return lax.broadcasted_iota(jnp.int32, shape, len(shape) - 1) < 64


def swap_halves(first, second):
    keep = low_half(first.shape)
    low = jnp.where(keep, first, pltpu.roll(second, 64, 1))
    high = jnp.where(keep, pltpu.roll(first, 64, 1), second)
    return low, high


def split(x):
    high = x.astype(bf16)
    return high, (x - high.astype(f32)).astype(bf16)


def split_table(x):
    high = x.astype(np.float32).astype(bf16)
    return high, (x - high.astype(np.float64)).astype(np.float32).astype(bf16)


def column_transform(x, high_ref, low_ref):
    high, low = split(x)
    both = mm(jnp.concatenate([high, low], axis=0), high_ref[...], precision=None)
    return both[:128] + both[128:] + mm(high, low_ref[...], precision=None)


def spread_body(data_ref, out_ref):
    flat = jnp.concatenate([data_ref[:, 0, :], data_ref[:, 1, :]], axis=1)
    two = jnp.concatenate([flat, flat], axis=0)
    for r in range(8):
        out_ref[r * 8 : r * 8 + 8, :] = two


def block_of_table(table_ref):
    return table_ref[lax.axis_index("x_hi"), lax.axis_index("z") * 2 + lax.axis_index("core")]


def spectra_body(data_ref, table_ref, out_ref):
    spectra = mm(block_of_table(table_ref), data_ref[...])
    for half in range(2):
        for r in range(8):
            out_ref[half, r] = spectra[half * 8 : half * 8 + 8, :]


def adjoint_body(gathered_ref, kernel_ref, scale_ref, high_ref, low_ref, out_ref, grid_ref):
    parts = [[], []]
    for j in range(4):
        first = gathered_ref[0, 2 * j] + gathered_ref[1, 2 * j]
        second = gathered_ref[0, 2 * j + 1] + gathered_ref[1, 2 * j + 1]
        low, high = swap_halves(first, second)
        parts[0].append(low)
        parts[1].append(high)
    rows = [jnp.concatenate(part, axis=1) for part in parts]
    sub = lax.broadcasted_iota(jnp.int32, (8, 512), 0)
    turned = [jnp.where(sub < 4, pltpu.roll(r, 4, 0), -pltpu.roll(r, 4, 0)) for r in rows]
    straight = jnp.concatenate(rows, axis=0)
    turned = jnp.concatenate(turned, axis=0)
    both = jnp.concatenate([straight, turned], axis=1)
    freq = lax.broadcasted_iota(jnp.int32, (16, 1024), 0) % 4
    total = None
    for k in range(4):
        left = jnp.where(freq == k, both, 0.0).astype(bf16)
        term = mm(left, kernel_ref[k].reshape(1024, 1024), precision=None)
        total = term if total is None else total + term
    row = lax.broadcasted_iota(jnp.int32, (16, 1024), 0) % 4
    scale = jnp.where(
        row < 2,
        jnp.where(row == 0, scale_ref[0], scale_ref[1]),
        jnp.where(row == 2, scale_ref[2], scale_ref[3]),
    )
    total = total * scale
    stack = jnp.concatenate([total[:, c * 128 : c * 128 + 128] for c in range(8)], axis=0)
    grid_ref[...] = column_transform(stack, high_ref, low_ref)
    for m in range(8):
        first = grid_ref[pl.ds(2 * m, 8, stride=16), :]
        second = grid_ref[pl.ds(2 * m + 1, 8, stride=16), :]
        tile = jnp.concatenate(swap_halves(first, second), axis=0).astype(bf16)
        for r in range(8):
            out_ref[r, :, m * 128 : m * 128 + 128] = tile


def images_body(
    grids_ref, kernel_ref, prior_ref, forward_ref, backward_ref, high_ref, low_ref, out_ref, grid_ref
):
    stripe = lax.axis_index("stripe")
    grids = grids_ref[...]
    modes = mm(forward_ref[...], jnp.concatenate([grids, grids], axis=0), precision=None)
    prior = prior_ref[...].T
    prior = jnp.concatenate([prior, prior], axis=1)
    modes = modes * jnp.concatenate([prior] * 8, axis=1)
    modes = jnp.concatenate(split(modes), axis=0)
    back = mm(backward_ref[stripe], modes, precision=None)
    back = back[0:16, :] + back[16:32, :]
    for m in range(8):
        first, second = swap_halves(
            back[0:8, m * 128 : m * 128 + 128], back[8:16, m * 128 : m * 128 + 128]
        )
        grid_ref[pl.ds(2 * m, 8, stride=16), :] = first
        grid_ref[pl.ds(2 * m + 1, 8, stride=16), :] = second
    smooth = column_transform(grid_ref[...], high_ref, low_ref)
    smooth = jnp.concatenate([smooth[c * 16 : c * 16 + 16, :] for c in range(8)], axis=1)
    left = smooth.astype(bf16)
    freq = lax.broadcasted_iota(jnp.int32, (16, 1024), 0) % 4
    total = None
    for k in range(4):
        term = None
        for c in range(4):
            right = kernel_ref[k, :, :, c * 256 : c * 256 + 256].reshape(1024, 256)
            piece = mm(left[:, c * 256 : c * 256 + 256], right, ((1,), (1,)), precision=None)
            term = piece if term is None else term + piece
        total = term if k == 0 else jnp.where(freq == k, term, total)
    sub = lax.broadcasted_iota(jnp.int32, (8, 512), 0)
    rows = []
    for n in range(2):
        moved = pltpu.roll(total[n * 8 : n * 8 + 8, 512:], 4, 0)
        rows.append(total[n * 8 : n * 8 + 8, :512] + jnp.where(sub < 4, -moved, moved))
    total = jnp.concatenate(rows, axis=0)
    for j in range(4):
        low, high = swap_halves(
            total[0:8, j * 128 : j * 128 + 128], total[8:16, j * 128 : j * 128 + 128]
        )
        low, high = low.astype(bf16), high.astype(bf16)
        for copy in range(4):
            out_ref[copy, 2 * j] = low
            out_ref[copy, 2 * j + 1] = high


def times_body(images_ref, table_ref, out_ref):
    half = lax.axis_index("x_hi") * 2 + lax.axis_index("core")
    blocks = []
    for block in range(4):
        total = images_ref[block, 0].astype(f32)
        for r in range(1, 8):
            total = total + images_ref[block, r].astype(f32)
        blocks.append(total)
    images = jnp.concatenate(blocks, axis=0)
    table = table_ref[lax.axis_index("z"), half]
    out_ref[...] = mm(table, images, ((0,), (0,)))


def finish_body(sums_ref, data_ref, noise_ref, out_ref):
    total = sums_ref[0:8, :]
    for r in range(1, 4):
        total = total + sums_ref[r * 8 : r * 8 + 8, :]
    total = total[0:4, :] + total[4:8, :]
    noise = noise_ref[...]
    out_ref[:, 0, :] = total[:, 0:64] + noise * data_ref[:, 0, :]
    out_ref[:, 1, :] = total[:, 64:128] + noise * data_ref[:, 1, :]


def exchange(x, axes):
    return lax.all_to_all(x, axes, 0, 0, tiled=True)


def shards(data_vec, kernel, time_spectrum, prior_spectrum, noise_var):
    table = jnp.asarray(fourier_table(2, 16))
    rows = sine_matrix(128)
    order = row_order()
    forward = jnp.asarray(np.concatenate(split_table(rows[:, order]), axis=1))
    high, low = split_table(rows[order].reshape(8, 16, 128))
    upper = np.concatenate([high, high], axis=2)
    lower = np.concatenate([low, np.zeros_like(low)], axis=2)
    backward = jnp.asarray(np.concatenate([upper, lower], axis=1))
    columns = [jnp.asarray(t) for t in split_table(np.kron(np.eye(2), sine_matrix(64)))]

    spread = call(
        spread_body,
        jax.ShapeDtypeStruct((64, 128), f32),
        (data_vec,),
        (whole(),),
        hint=2e10,
    )
    by_time = exchange(spread.reshape(16, 4, 128), ("z", "core")).reshape(64, 128)
    spectra = call(
        spectra_body,
        jax.ShapeDtypeStruct((2, 8, 8, 128), f32),
        (by_time, table),
        (whole(), whole()),
        hint=2e10,
    )
    gathered = exchange(spectra.reshape(16, 8, 128), ("x_hi", "stripe"))
    grids = call(
        adjoint_body,
        jax.ShapeDtypeStruct((8, 16, 1024), bf16),
        (gathered.reshape(2, 8, 8, 128), kernel, time_spectrum, *columns),
        (whole(), whole(), scalars(), whole(), whole()),
        (pltpu.VMEM((128, 128), f32),),
        limit=20 << 20,
    )
    grids = exchange(grids, "stripe").reshape(128, 1024)
    images = call(
        images_body,
        jax.ShapeDtypeStruct((4, 8, 8, 128), bf16),
        (grids, kernel, prior_spectrum.T, forward, backward, *columns),
        (whole(),) * 7,
        (pltpu.VMEM((128, 128), f32),),
        limit=20 << 20,
    )
    images = exchange(images.reshape(32, 8, 128), ("x_hi", "core", "stripe"))
    sums = call(
        times_body,
        jax.ShapeDtypeStruct((32, 128), f32),
        (images.reshape(4, 8, 8, 128), jnp.asarray(inverse_table())),
        (whole(), whole()),
    )
    sums = exchange(sums.reshape(8, 4, 128), "z").reshape(32, 128)
    return call(
        finish_body,
        jax.ShapeDtypeStruct((4, 2, 64), f32),
        (sums, data_vec, noise_var.reshape(1, 64)),
        (whole(),) * 3,
    )


def solution(mesh):
    fine = Mesh(mesh.devices.reshape(2, 8, 2, 8), ("x_hi", "z", "core", "stripe"))
    tm = ("x_hi", "z", "core")
    return jax.shard_map(
        shards,
        mesh=fine,
        in_specs=(
            P(tm, None, "stripe"),
            P(tm, None, None, "stripe"),
            P(tm),
            P(),
            P("stripe"),
        ),
        out_specs=P(tm, None, "stripe"),
        check_vma=False,
    )
```

```python
import math

import jax
import jax.numpy as jnp
import numpy as np
from jax import lax
from jax.experimental import pallas as pl
from jax.experimental.pallas import tpu as pltpu
from jax.sharding import Mesh
from jax.sharding import PartitionSpec as P

f32 = jnp.float32
bf16 = jnp.bfloat16


def whole():
    return pl.BlockSpec(memory_space=pltpu.VMEM)


def call(body, out_shape, operands, specs, scratch=(), limit=4 << 20, hint=1e6):
    return pl.pallas_call(
        body,
        out_shape=out_shape,
        in_specs=list(specs),
        out_specs=whole(),
        scratch_shapes=list(scratch),
        cost_estimate=pl.CostEstimate(
            flops=int(hint), transcendentals=0, bytes_accessed=100_000
        ),
        compiler_params=pltpu.CompilerParams(vmem_limit_bytes=limit),
    )(*operands)


def mm(a, b, dims=((1,), (0,))):
    return lax.dot_general(
        a, b, (dims, ((), ())), preferred_element_type=f32
    )


def fourier_table(halves, blocks):
    steps = np.arange(128)
    angles = np.outer(steps, steps) % 256 * (math.pi / 128)
    pair = np.stack([np.cos(angles), -np.sin(angles)]) / math.sqrt(128)
    pair = pair.reshape(2, halves, blocks, 4, halves, 64).transpose(4, 2, 1, 0, 3, 5)
    return triple_table(pair.reshape(halves, blocks, halves * 8, 64))


def inverse_table():
    steps = np.arange(128)
    angles = np.outer(steps, steps) % 256 * (math.pi / 128)
    pair = np.stack([np.cos(angles), -np.sin(angles)]) / math.sqrt(128)
    pair = pair.reshape(2, 2, 8, 2, 4, 2, 8, 2, 4)
    pair = pair.transpose(2, 5, 7, 6, 8, 1, 3, 0, 4)
    return triple_table(pair.reshape(8, 4, 32, 32))


def sine_matrix(length):
    numbers = np.arange(length) + 1
    product = np.outer(numbers, numbers) % (2 * (length + 1))
    return np.sin(product * (math.pi / (length + 1))) * math.sqrt(2.0 / (length + 1))


def row_order():
    stripe, parity, c = np.meshgrid(np.arange(8), np.arange(2), np.arange(8), indexing="ij")
    return (stripe * 16 + 2 * c + parity).reshape(-1)


def low_half(shape):
    return lax.broadcasted_iota(jnp.int32, shape, len(shape) - 1) < 64


def swap_halves(first, second):
    keep = low_half(first.shape)
    low = jnp.where(keep, first, pltpu.roll(second, 64, 1))
    high = jnp.where(keep, pltpu.roll(first, 64, 1), second)
    return low, high


def split(x):
    high = x.astype(bf16)
    return high, (x - high.astype(f32)).astype(bf16)


def split_table(x):
    high = x.astype(np.float32).astype(bf16)
    return high, (x - high.astype(np.float64)).astype(np.float32).astype(bf16)


def triple_table(x):
    high, low = split_table(x)
    return np.concatenate([high, high, low], axis=-1)


def triple_product(table, x):
    high, low = split(x)
    return mm(table, jnp.concatenate([high, low, high], axis=0))


def column_transform(x, high_ref, low_ref):
    high, low = split(x)
    both = mm(jnp.concatenate([high, low], axis=0), high_ref[...])
    return both[:128] + both[128:] + mm(high, low_ref[...])


def spread_body(data_ref, out_ref):
    flat = jnp.concatenate([data_ref[:, 0, :], data_ref[:, 1, :]], axis=1)
    two = jnp.concatenate([flat, flat], axis=0)
    for r in range(8):
        out_ref[r * 8 : r * 8 + 8, :] = two


def block_of_table(table_ref):
    return table_ref[lax.axis_index("x_hi"), lax.axis_index("z") * 2 + lax.axis_index("core")]


def spectra_body(data_ref, table_ref, out_ref):
    spectra = triple_product(block_of_table(table_ref), data_ref[...])
    for half in range(2):
        for r in range(8):
            out_ref[half, r] = spectra[half * 8 : half * 8 + 8, :]


def adjoint_body(gathered_ref, kernel_ref, scale_ref, high_ref, low_ref, out_ref, grid_ref):
    parts = [[], []]
    for j in range(4):
        first = gathered_ref[0, 2 * j] + gathered_ref[1, 2 * j]
        second = gathered_ref[0, 2 * j + 1] + gathered_ref[1, 2 * j + 1]
        low, high = swap_halves(first, second)
        parts[0].append(low)
        parts[1].append(high)
    rows = [jnp.concatenate(part, axis=1) for part in parts]
    sub = lax.broadcasted_iota(jnp.int32, (8, 512), 0)
    turned = [jnp.where(sub < 4, pltpu.roll(r, 4, 0), -pltpu.roll(r, 4, 0)) for r in rows]
    straight = jnp.concatenate(rows, axis=0)
    turned = jnp.concatenate(turned, axis=0)
    both = jnp.concatenate([straight, turned], axis=1)
    freq = lax.broadcasted_iota(jnp.int32, (16, 1024), 0) % 4
    total = None
    for k in range(4):
        left = jnp.where(freq == k, both, 0.0).astype(bf16)
        term = mm(left, kernel_ref[k].reshape(1024, 1024))
        total = term if total is None else total + term
    row = lax.broadcasted_iota(jnp.int32, (16, 128), 0) % 4
    scale = jnp.broadcast_to(scale_ref[0:1, 0:1], (16, 128))
    for k in range(1, 4):
        scale = jnp.where(row == k, scale_ref[0:1, k : k + 1], scale)
    scale = jnp.concatenate([scale] * 8, axis=1)
    total = total * scale
    stack = jnp.concatenate([total[:, c * 128 : c * 128 + 128] for c in range(8)], axis=0)
    grid_ref[...] = column_transform(stack, high_ref, low_ref)
    for m in range(8):
        first = grid_ref[pl.ds(2 * m, 8, stride=16), :]
        second = grid_ref[pl.ds(2 * m + 1, 8, stride=16), :]
        tile = jnp.concatenate(swap_halves(first, second), axis=0).astype(bf16)
        for r in range(8):
            out_ref[r, :, m * 128 : m * 128 + 128] = tile


def images_body(
    grids_ref, kernel_ref, prior_ref, forward_ref, backward_ref, high_ref, low_ref, out_ref, grid_ref
):
    stripe = lax.axis_index("stripe")
    grids = grids_ref[...]
    modes = mm(forward_ref[...], jnp.concatenate([grids, grids], axis=0))
    prior = prior_ref[...].T
    prior = jnp.concatenate([prior, prior], axis=1)
    modes = modes * jnp.concatenate([prior] * 8, axis=1)
    modes = jnp.concatenate(split(modes), axis=0)
    back = mm(backward_ref[stripe], modes)
    back = back[0:16, :] + back[16:32, :]
    for m in range(8):
        first, second = swap_halves(
            back[0:8, m * 128 : m * 128 + 128], back[8:16, m * 128 : m * 128 + 128]
        )
        grid_ref[pl.ds(2 * m, 8, stride=16), :] = first
        grid_ref[pl.ds(2 * m + 1, 8, stride=16), :] = second
    smooth = column_transform(grid_ref[...], high_ref, low_ref)
    smooth = jnp.concatenate([smooth[c * 16 : c * 16 + 16, :] for c in range(8)], axis=1)
    left = smooth.astype(bf16)
    freq = lax.broadcasted_iota(jnp.int32, (16, 1024), 0) % 4
    total = None
    for k in range(4):
        term = None
        for c in range(4):
            right = kernel_ref[k, :, :, c * 256 : c * 256 + 256].reshape(1024, 256)
            piece = mm(left[:, c * 256 : c * 256 + 256], right, ((1,), (1,)))
            term = piece if term is None else term + piece
        total = term if k == 0 else jnp.where(freq == k, term, total)
    sub = lax.broadcasted_iota(jnp.int32, (8, 512), 0)
    rows = []
    for n in range(2):
        moved = pltpu.roll(total[n * 8 : n * 8 + 8, 512:], 4, 0)
        rows.append(total[n * 8 : n * 8 + 8, :512] + jnp.where(sub < 4, -moved, moved))
    total = jnp.concatenate(rows, axis=0)
    for j in range(4):
        low, high = swap_halves(
            total[0:8, j * 128 : j * 128 + 128], total[8:16, j * 128 : j * 128 + 128]
        )
        low, high = low.astype(bf16), high.astype(bf16)
        for copy in range(4):
            out_ref[copy, 2 * j] = low
            out_ref[copy, 2 * j + 1] = high


def times_body(images_ref, table_ref, out_ref):
    half = lax.axis_index("x_hi") * 2 + lax.axis_index("core")
    blocks = []
    for block in range(4):
        total = images_ref[block, 0].astype(f32)
        for r in range(1, 8):
            total = total + images_ref[block, r].astype(f32)
        blocks.append(total)
    images = jnp.concatenate(blocks, axis=0)
    table = table_ref[lax.axis_index("z"), half]
    out_ref[...] = triple_product(table, images)


def finish_body(sums_ref, data_ref, noise_ref, out_ref):
    total = sums_ref[0:8, :]
    for r in range(1, 4):
        total = total + sums_ref[r * 8 : r * 8 + 8, :]
    total = total[0:4, :] + total[4:8, :]
    noise = noise_ref[...]
    out_ref[:, 0, :] = total[:, 0:64] + noise * data_ref[:, 0, :]
    out_ref[:, 1, :] = total[:, 64:128] + noise * data_ref[:, 1, :]


def exchange(x, axes):
    return lax.all_to_all(x, axes, 0, 0, tiled=True)


def shards(data_vec, kernel, time_spectrum, prior_spectrum, noise_var):
    table = jnp.asarray(fourier_table(2, 16))
    rows = sine_matrix(128)
    order = row_order()
    forward = jnp.asarray(np.concatenate(split_table(rows[:, order]), axis=1))
    high, low = split_table(rows[order].reshape(8, 16, 128))
    upper = np.concatenate([high, high], axis=2)
    lower = np.concatenate([low, np.zeros_like(low)], axis=2)
    backward = jnp.asarray(np.concatenate([upper, lower], axis=1))
    columns = [jnp.asarray(t) for t in split_table(np.kron(np.eye(2), sine_matrix(64)))]

    spread = call(
        spread_body,
        jax.ShapeDtypeStruct((64, 128), f32),
        (data_vec,),
        (whole(),),
        hint=2e10,
    )
    by_time = exchange(spread.reshape(16, 4, 128), ("z", "core")).reshape(64, 128)
    spectra = call(
        spectra_body,
        jax.ShapeDtypeStruct((2, 8, 8, 128), f32),
        (by_time, table),
        (whole(), whole()),
        hint=2e10,
    )
    gathered = exchange(spectra.reshape(16, 8, 128), ("x_hi", "stripe"))
    grids = call(
        adjoint_body,
        jax.ShapeDtypeStruct((8, 16, 1024), bf16),
        (gathered.reshape(2, 8, 8, 128), kernel, time_spectrum.reshape(1, 4), *columns),
        (whole(),) * 5,
        (pltpu.VMEM((128, 128), f32),),
        limit=20 << 20,
    )
    grids = exchange(grids, "stripe").reshape(128, 1024)
    images = call(
        images_body,
        jax.ShapeDtypeStruct((4, 8, 8, 128), bf16),
        (grids, kernel, prior_spectrum.T, forward, backward, *columns),
        (whole(),) * 7,
        (pltpu.VMEM((128, 128), f32),),
        limit=20 << 20,
    )
    images = exchange(images.reshape(32, 8, 128), ("x_hi", "core", "stripe"))
    sums = call(
        times_body,
        jax.ShapeDtypeStruct((32, 128), f32),
        (images.reshape(4, 8, 8, 128), jnp.asarray(inverse_table())),
        (whole(), whole()),
    )
    sums = exchange(sums.reshape(8, 4, 128), "z").reshape(32, 128)
    return call(
        finish_body,
        jax.ShapeDtypeStruct((4, 2, 64), f32),
        (sums, data_vec, noise_var.reshape(1, 64)),
        (whole(),) * 3,
    )


def solution(mesh):
    fine = Mesh(mesh.devices.reshape(2, 8, 2, 8), ("x_hi", "z", "core", "stripe"))
    tm = ("x_hi", "z", "core")
    return jax.shard_map(
        shards,
        mesh=fine,
        in_specs=(
            P(tm, None, "stripe"),
            P(tm, None, None, "stripe"),
            P(tm),
            P(),
            P("stripe"),
        ),
        out_specs=P(tm, None, "stripe"),
        check_vma=False,
    )
```

```python
import math

import jax
import jax.numpy as jnp
import numpy as np
from jax import lax
from jax.experimental import pallas as pl
from jax.experimental.pallas import tpu as pltpu
from jax.sharding import Mesh
from jax.sharding import PartitionSpec as P

f32 = jnp.float32
bf16 = jnp.bfloat16


def whole():
    return pl.BlockSpec(memory_space=pltpu.VMEM)


def call(body, out_shape, operands, specs, scratch=(), limit=4 << 20, hint=1e6):
    return pl.pallas_call(
        body,
        out_shape=out_shape,
        in_specs=list(specs),
        out_specs=whole(),
        scratch_shapes=list(scratch),
        cost_estimate=pl.CostEstimate(
            flops=int(hint), transcendentals=0, bytes_accessed=100_000
        ),
        compiler_params=pltpu.CompilerParams(vmem_limit_bytes=limit),
    )(*operands)


def mm(a, b, dims=((1,), (0,))):
    return lax.dot_general(
        a, b, (dims, ((), ())), preferred_element_type=f32
    )


def fourier_table(halves, blocks):
    steps = np.arange(128)
    angles = np.outer(steps, steps) % 256 * (math.pi / 128)
    pair = np.stack([np.cos(angles), -np.sin(angles)]) / math.sqrt(128)
    pair = pair.reshape(2, halves, blocks, 4, halves, 64).transpose(4, 2, 1, 0, 3, 5)
    return triple_table(pair.reshape(halves, blocks, halves * 8, 64))


def inverse_table():
    steps = np.arange(128)
    angles = np.outer(steps, steps) % 256 * (math.pi / 128)
    pair = np.stack([np.cos(angles), -np.sin(angles)]) / math.sqrt(128)
    pair = pair.reshape(2, 2, 8, 2, 4, 2, 8, 2, 4)
    pair = pair.transpose(2, 5, 7, 6, 8, 1, 3, 0, 4)
    return triple_table(pair.reshape(8, 4, 32, 32))


def sine_matrix(length):
    numbers = np.arange(length) + 1
    product = np.outer(numbers, numbers) % (2 * (length + 1))
    return np.sin(product * (math.pi / (length + 1))) * math.sqrt(2.0 / (length + 1))


def row_order():
    stripe, parity, c = np.meshgrid(np.arange(8), np.arange(2), np.arange(8), indexing="ij")
    return (stripe * 16 + 2 * c + parity).reshape(-1)


def low_half(shape):
    return lax.broadcasted_iota(jnp.int32, shape, len(shape) - 1) < 64


def swap_halves(first, second):
    keep = low_half(first.shape)
    low = jnp.where(keep, first, pltpu.roll(second, 64, 1))
    high = jnp.where(keep, pltpu.roll(first, 64, 1), second)
    return low, high


def split(x):
    high = x.astype(bf16)
    return high, (x - high.astype(f32)).astype(bf16)


def split_table(x):
    high = x.astype(np.float32).astype(bf16)
    return high, (x - high.astype(np.float64)).astype(np.float32).astype(bf16)


def triple_table(x):
    high, low = split_table(x)
    return np.concatenate([high, high, low], axis=-1)


def triple_product(table, x):
    high, low = split(x)
    return mm(table, jnp.concatenate([high, low, high], axis=0))


def column_transform(x, high_ref, low_ref):
    high, low = split(x)
    both = mm(jnp.concatenate([high, low], axis=0), high_ref[...])
    return both[:128] + both[128:] + mm(high, low_ref[...])


def spread_body(data_ref, out_ref):
    flat = jnp.concatenate([data_ref[:, 0, :], data_ref[:, 1, :]], axis=1)
    two = jnp.concatenate([flat, flat], axis=0)
    for r in range(8):
        out_ref[r * 8 : r * 8 + 8, :] = two


def block_of_table(table_ref):
    return table_ref[lax.axis_index("x_hi"), lax.axis_index("z") * 2 + lax.axis_index("core")]


def spectra_body(data_ref, table_ref, out_ref):
    spectra = triple_product(block_of_table(table_ref), data_ref[...])
    for half in range(2):
        for r in range(8):
            out_ref[half, r] = spectra[half * 8 : half * 8 + 8, :]


def adjoint_body(gathered_ref, kernel_ref, scale_ref, high_ref, low_ref, out_ref, grid_ref):
    parts = [[], []]
    for j in range(4):
        first = gathered_ref[0, 2 * j] + gathered_ref[1, 2 * j]
        second = gathered_ref[0, 2 * j + 1] + gathered_ref[1, 2 * j + 1]
        low, high = swap_halves(first, second)
        parts[0].append(low)
        parts[1].append(high)
    rows = [jnp.concatenate(part, axis=1) for part in parts]
    sub = lax.broadcasted_iota(jnp.int32, (8, 512), 0)
    turned = [jnp.where(sub < 4, pltpu.roll(r, 4, 0), -pltpu.roll(r, 4, 0)) for r in rows]
    straight = jnp.concatenate(rows, axis=0)
    turned = jnp.concatenate(turned, axis=0)
    both = jnp.concatenate([straight, turned], axis=1)
    freq = lax.broadcasted_iota(jnp.int32, (16, 1024), 0) % 4
    total = None
    for k in range(4):
        left = jnp.where(freq == k, both, 0.0).astype(bf16)
        term = mm(left, kernel_ref[k].reshape(1024, 1024))
        total = term if total is None else total + term
    row = lax.broadcasted_iota(jnp.int32, (16, 128), 0) % 4
    scale = jnp.broadcast_to(scale_ref[0:1, 0:1], (16, 128))
    for k in range(1, 4):
        scale = jnp.where(row == k, scale_ref[0:1, k : k + 1], scale)
    scale = jnp.concatenate([scale] * 8, axis=1)
    total = total * scale
    stack = jnp.concatenate([total[:, c * 128 : c * 128 + 128] for c in range(8)], axis=0)
    grid_ref[...] = column_transform(stack, high_ref, low_ref)
    for m in range(8):
        first = grid_ref[pl.ds(2 * m, 8, stride=16), :]
        second = grid_ref[pl.ds(2 * m + 1, 8, stride=16), :]
        tile = jnp.concatenate(swap_halves(first, second), axis=0).astype(bf16)
        for r in range(8):
            out_ref[r, :, m * 128 : m * 128 + 128] = tile


def images_body(
    grids_ref, kernel_ref, prior_ref, forward_ref, backward_ref, high_ref, low_ref, out_ref, grid_ref, turned_ref
):
    stripe = lax.axis_index("stripe")
    for row in range(0, 1024, 512):
        for column in range(0, 1024, 512):
            tile = kernel_ref[3, row // 512, row % 512 : row % 512 + 512, column : column + 512]
            turned_ref[column : column + 512, row : row + 512] = tile.T
    grids = grids_ref[...]
    modes = mm(forward_ref[...], jnp.concatenate([grids, grids], axis=0))
    prior = prior_ref[...].T
    prior = jnp.concatenate([prior, prior], axis=1)
    modes = modes * jnp.concatenate([prior] * 8, axis=1)
    modes = jnp.concatenate(split(modes), axis=0)
    back = mm(backward_ref[stripe], modes)
    back = back[0:16, :] + back[16:32, :]
    for m in range(8):
        first, second = swap_halves(
            back[0:8, m * 128 : m * 128 + 128], back[8:16, m * 128 : m * 128 + 128]
        )
        grid_ref[pl.ds(2 * m, 8, stride=16), :] = first
        grid_ref[pl.ds(2 * m + 1, 8, stride=16), :] = second
    smooth = column_transform(grid_ref[...], high_ref, low_ref)
    smooth = jnp.concatenate([smooth[c * 16 : c * 16 + 16, :] for c in range(8)], axis=1)
    left = smooth.astype(bf16)
    freq = lax.broadcasted_iota(jnp.int32, (16, 1024), 0) % 4
    total = None
    for k in range(4):
        if k == 3:
            term = mm(left, turned_ref[...])
        else:
            term = None
            for c in range(4):
                right = kernel_ref[k, :, :, c * 256 : c * 256 + 256].reshape(1024, 256)
                piece = mm(left[:, c * 256 : c * 256 + 256], right, ((1,), (1,)))
                term = piece if term is None else term + piece
        total = term if k == 0 else jnp.where(freq == k, term, total)
    sub = lax.broadcasted_iota(jnp.int32, (8, 512), 0)
    rows = []
    for n in range(2):
        moved = pltpu.roll(total[n * 8 : n * 8 + 8, 512:], 4, 0)
        rows.append(total[n * 8 : n * 8 + 8, :512] + jnp.where(sub < 4, -moved, moved))
    total = jnp.concatenate(rows, axis=0)
    for j in range(4):
        low, high = swap_halves(
            total[0:8, j * 128 : j * 128 + 128], total[8:16, j * 128 : j * 128 + 128]
        )
        low, high = low.astype(bf16), high.astype(bf16)
        for copy in range(4):
            out_ref[copy, 2 * j] = low
            out_ref[copy, 2 * j + 1] = high


def times_body(images_ref, table_ref, out_ref):
    half = lax.axis_index("x_hi") * 2 + lax.axis_index("core")
    blocks = []
    for block in range(4):
        total = images_ref[block, 0].astype(f32)
        for r in range(1, 8):
            total = total + images_ref[block, r].astype(f32)
        blocks.append(total)
    images = jnp.concatenate(blocks, axis=0)
    table = table_ref[lax.axis_index("z"), half]
    out_ref[...] = triple_product(table, images)


def finish_body(sums_ref, data_ref, noise_ref, out_ref):
    total = sums_ref[0:8, :]
    for r in range(1, 4):
        total = total + sums_ref[r * 8 : r * 8 + 8, :]
    total = total[0:4, :] + total[4:8, :]
    noise = noise_ref[...]
    out_ref[:, 0, :] = total[:, 0:64] + noise * data_ref[:, 0, :]
    out_ref[:, 1, :] = total[:, 64:128] + noise * data_ref[:, 1, :]


def exchange(x, axes):
    return lax.all_to_all(x, axes, 0, 0, tiled=True)


def shards(data_vec, kernel, time_spectrum, prior_spectrum, noise_var):
    table = jnp.asarray(fourier_table(2, 16))
    rows = sine_matrix(128)
    order = row_order()
    forward = jnp.asarray(np.concatenate(split_table(rows[:, order]), axis=1))
    high, low = split_table(rows[order].reshape(8, 16, 128))
    upper = np.concatenate([high, high], axis=2)
    lower = np.concatenate([low, np.zeros_like(low)], axis=2)
    backward = jnp.asarray(np.concatenate([upper, lower], axis=1))
    columns = [jnp.asarray(t) for t in split_table(np.kron(np.eye(2), sine_matrix(64)))]

    spread = call(
        spread_body,
        jax.ShapeDtypeStruct((64, 128), f32),
        (data_vec,),
        (whole(),),
        hint=2e10,
    )
    by_time = exchange(spread.reshape(16, 4, 128), ("z", "core")).reshape(64, 128)
    spectra = call(
        spectra_body,
        jax.ShapeDtypeStruct((2, 8, 8, 128), f32),
        (by_time, table),
        (whole(), whole()),
        hint=2e10,
    )
    gathered = exchange(spectra.reshape(16, 8, 128), ("x_hi", "stripe"))
    grids = call(
        adjoint_body,
        jax.ShapeDtypeStruct((8, 16, 1024), bf16),
        (gathered.reshape(2, 8, 8, 128), kernel, time_spectrum.reshape(1, 4), *columns),
        (whole(),) * 5,
        (pltpu.VMEM((128, 128), f32),),
        limit=20 << 20,
    )
    grids = exchange(grids, "stripe").reshape(128, 1024)
    images = call(
        images_body,
        jax.ShapeDtypeStruct((4, 8, 8, 128), bf16),
        (grids, kernel, prior_spectrum.T, forward, backward, *columns),
        (whole(),) * 7,
        (pltpu.VMEM((128, 128), f32), pltpu.VMEM((1024, 1024), bf16)),
        limit=20 << 20,
    )
    images = exchange(images.reshape(32, 8, 128), ("x_hi", "core", "stripe"))
    sums = call(
        times_body,
        jax.ShapeDtypeStruct((32, 128), f32),
        (images.reshape(4, 8, 8, 128), jnp.asarray(inverse_table())),
        (whole(), whole()),
    )
    sums = exchange(sums.reshape(8, 4, 128), "z").reshape(32, 128)
    return call(
        finish_body,
        jax.ShapeDtypeStruct((4, 2, 64), f32),
        (sums, data_vec, noise_var.reshape(1, 64)),
        (whole(),) * 3,
    )


def solution(mesh):
    fine = Mesh(mesh.devices.reshape(2, 8, 2, 8), ("x_hi", "z", "core", "stripe"))
    tm = ("x_hi", "z", "core")
    return jax.shard_map(
        shards,
        mesh=fine,
        in_specs=(
            P(tm, None, "stripe"),
            P(tm, None, None, "stripe"),
            P(tm),
            P(),
            P("stripe"),
        ),
        out_specs=P(tm, None, "stripe"),
        check_vma=False,
    )
```

```python
import math

import jax
import jax.numpy as jnp
import numpy as np
from jax import lax
from jax.experimental import pallas as pl
from jax.experimental.pallas import tpu as pltpu
from jax.sharding import Mesh
from jax.sharding import PartitionSpec as P

f32 = jnp.float32
bf16 = jnp.bfloat16


def whole():
    return pl.BlockSpec(memory_space=pltpu.VMEM)


def call(body, out_shape, operands, specs, scratch=(), limit=4 << 20, hint=1e6):
    return pl.pallas_call(
        body,
        out_shape=out_shape,
        in_specs=list(specs),
        out_specs=whole(),
        scratch_shapes=list(scratch),
        cost_estimate=pl.CostEstimate(
            flops=int(hint), transcendentals=0, bytes_accessed=100_000
        ),
        compiler_params=pltpu.CompilerParams(vmem_limit_bytes=limit),
    )(*operands)


def mm(a, b, dims=((1,), (0,))):
    return lax.dot_general(
        a, b, (dims, ((), ())), preferred_element_type=f32
    )


def fourier_table(halves, blocks):
    steps = np.arange(128)
    angles = np.outer(steps, steps) % 256 * (math.pi / 128)
    pair = np.stack([np.cos(angles), -np.sin(angles)]) / math.sqrt(128)
    pair = pair.reshape(2, halves, blocks, 4, halves, 64).transpose(4, 2, 1, 0, 3, 5)
    return triple_table(pair.reshape(halves, blocks, halves * 8, 64))


def inverse_table():
    steps = np.arange(128)
    angles = np.outer(steps, steps) % 256 * (math.pi / 128)
    pair = np.stack([np.cos(angles), -np.sin(angles)]) / math.sqrt(128)
    pair = pair.reshape(2, 2, 8, 2, 4, 2, 8, 2, 4)
    pair = pair.transpose(2, 5, 7, 6, 8, 1, 3, 0, 4)
    return triple_table(pair.reshape(8, 4, 32, 32))


def sine_matrix(length):
    numbers = np.arange(length) + 1
    product = np.outer(numbers, numbers) % (2 * (length + 1))
    return np.sin(product * (math.pi / (length + 1))) * math.sqrt(2.0 / (length + 1))


def row_order():
    stripe, parity, c = np.meshgrid(np.arange(8), np.arange(2), np.arange(8), indexing="ij")
    return (stripe * 16 + 2 * c + parity).reshape(-1)


def low_half(shape):
    return lax.broadcasted_iota(jnp.int32, shape, len(shape) - 1) < 64


def swap_halves(first, second):
    keep = low_half(first.shape)
    low = jnp.where(keep, first, pltpu.roll(second, 64, 1))
    high = jnp.where(keep, pltpu.roll(first, 64, 1), second)
    return low, high


def split(x):
    high = x.astype(bf16)
    return high, (x - high.astype(f32)).astype(bf16)


def split_table(x):
    high = x.astype(np.float32).astype(bf16)
    return high, (x - high.astype(np.float64)).astype(np.float32).astype(bf16)


def triple_table(x):
    high, low = split_table(x)
    return np.concatenate([high, high, low], axis=-1)


def triple_product(table, x):
    high, low = split(x)
    return mm(table, jnp.concatenate([high, low, high], axis=0))


def column_transform(x, high_ref, low_ref):
    high, low = split(x)
    both = mm(jnp.concatenate([high, low], axis=0), high_ref[...])
    return both[:128] + both[128:] + mm(high, low_ref[...])


def spread_body(data_ref, out_ref):
    flat = jnp.concatenate([data_ref[:, 0, :], data_ref[:, 1, :]], axis=1)
    two = jnp.concatenate([flat, flat], axis=0)
    for r in range(8):
        out_ref[r * 8 : r * 8 + 8, :] = two


def block_of_table(table_ref):
    return table_ref[lax.axis_index("x_hi"), lax.axis_index("z") * 2 + lax.axis_index("core")]


def spectra_body(data_ref, table_ref, out_ref):
    spectra = triple_product(block_of_table(table_ref), data_ref[...])
    for half in range(2):
        for r in range(8):
            out_ref[half, r] = spectra[half * 8 : half * 8 + 8, :]


def adjoint_body(gathered_ref, kernel_ref, scale_ref, high_ref, low_ref, out_ref, grid_ref):
    parts = [[], []]
    for j in range(4):
        first = gathered_ref[0, 2 * j] + gathered_ref[1, 2 * j]
        second = gathered_ref[0, 2 * j + 1] + gathered_ref[1, 2 * j + 1]
        low, high = swap_halves(first, second)
        parts[0].append(low)
        parts[1].append(high)
    rows = [jnp.concatenate(part, axis=1) for part in parts]
    sub = lax.broadcasted_iota(jnp.int32, (8, 512), 0)
    turned = [jnp.where(sub < 4, pltpu.roll(r, 4, 0), -pltpu.roll(r, 4, 0)) for r in rows]
    straight = jnp.concatenate(rows, axis=0)
    turned = jnp.concatenate(turned, axis=0)
    both = jnp.concatenate([straight, turned], axis=1)
    freq = lax.broadcasted_iota(jnp.int32, (16, 1024), 0) % 4
    total = None
    for k in range(4):
        left = jnp.where(freq == k, both, 0.0).astype(bf16)
        term = mm(left, kernel_ref[k].reshape(1024, 1024))
        total = term if total is None else total + term
    row = lax.broadcasted_iota(jnp.int32, (16, 128), 0) % 4
    scale = jnp.broadcast_to(scale_ref[0:1, 0:1], (16, 128))
    for k in range(1, 4):
        scale = jnp.where(row == k, scale_ref[0:1, k : k + 1], scale)
    scale = jnp.concatenate([scale] * 8, axis=1)
    total = total * scale
    stack = jnp.concatenate([total[:, c * 128 : c * 128 + 128] for c in range(8)], axis=0)
    grid_ref[...] = column_transform(stack, high_ref, low_ref)
    for m in range(8):
        first = grid_ref[pl.ds(2 * m, 8, stride=16), :]
        second = grid_ref[pl.ds(2 * m + 1, 8, stride=16), :]
        tile = jnp.concatenate(swap_halves(first, second), axis=0).astype(bf16)
        for r in range(8):
            out_ref[r, :, m * 128 : m * 128 + 128] = tile


def images_body(
    grids_ref, kernel_ref, prior_ref, forward_ref, backward_ref, high_ref, low_ref, out_ref, grid_ref, turned_ref
):
    stripe = lax.axis_index("stripe")
    for c in range(3):
        for column in range(0, 1024, 512):
            tile = kernel_ref[(c + 5) // 2, (c + 1) % 2, :, column : column + 512]
            turned_ref[column : column + 512, c * 512 : c * 512 + 512] = tile.T
    grids = grids_ref[...]
    modes = mm(forward_ref[...], jnp.concatenate([grids, grids], axis=0))
    prior = prior_ref[...].T
    prior = jnp.concatenate([prior, prior], axis=1)
    modes = modes * jnp.concatenate([prior] * 8, axis=1)
    modes = jnp.concatenate(split(modes), axis=0)
    back = mm(backward_ref[stripe], modes)
    back = back[0:16, :] + back[16:32, :]
    for m in range(8):
        first, second = swap_halves(
            back[0:8, m * 128 : m * 128 + 128], back[8:16, m * 128 : m * 128 + 128]
        )
        grid_ref[pl.ds(2 * m, 8, stride=16), :] = first
        grid_ref[pl.ds(2 * m + 1, 8, stride=16), :] = second
    smooth = column_transform(grid_ref[...], high_ref, low_ref)
    smooth = jnp.concatenate([smooth[c * 16 : c * 16 + 16, :] for c in range(8)], axis=1)
    left = smooth.astype(bf16)
    freq = lax.broadcasted_iota(jnp.int32, (16, 1024), 0) % 4
    total = None
    for k in range(4):
        if k == 3:
            term = mm(left, turned_ref[:, 512:])
        elif k == 2:
            term = None
            for c in range(4):
                right = kernel_ref[k, 0, :, c * 256 : c * 256 + 256]
                piece = mm(left[:, c * 256 : c * 256 + 256], right, ((1,), (1,)))
                term = piece if term is None else term + piece
            term = jnp.concatenate([term, mm(left, turned_ref[:, :512])], axis=1)
        else:
            term = None
            for c in range(4):
                right = kernel_ref[k, :, :, c * 256 : c * 256 + 256].reshape(1024, 256)
                piece = mm(left[:, c * 256 : c * 256 + 256], right, ((1,), (1,)))
                term = piece if term is None else term + piece
        total = term if k == 0 else jnp.where(freq == k, term, total)
    sub = lax.broadcasted_iota(jnp.int32, (8, 512), 0)
    rows = []
    for n in range(2):
        moved = pltpu.roll(total[n * 8 : n * 8 + 8, 512:], 4, 0)
        rows.append(total[n * 8 : n * 8 + 8, :512] + jnp.where(sub < 4, -moved, moved))
    total = jnp.concatenate(rows, axis=0)
    for j in range(4):
        low, high = swap_halves(
            total[0:8, j * 128 : j * 128 + 128], total[8:16, j * 128 : j * 128 + 128]
        )
        low, high = low.astype(bf16), high.astype(bf16)
        for copy in range(4):
            out_ref[copy, 2 * j] = low
            out_ref[copy, 2 * j + 1] = high


def times_body(images_ref, table_ref, out_ref):
    half = lax.axis_index("x_hi") * 2 + lax.axis_index("core")
    blocks = []
    for block in range(4):
        total = images_ref[block, 0].astype(f32)
        for r in range(1, 8):
            total = total + images_ref[block, r].astype(f32)
        blocks.append(total)
    images = jnp.concatenate(blocks, axis=0)
    table = table_ref[lax.axis_index("z"), half]
    out_ref[...] = triple_product(table, images)


def finish_body(sums_ref, data_ref, noise_ref, out_ref):
    total = sums_ref[0:8, :]
    for r in range(1, 4):
        total = total + sums_ref[r * 8 : r * 8 + 8, :]
    total = total[0:4, :] + total[4:8, :]
    noise = noise_ref[...]
    out_ref[:, 0, :] = total[:, 0:64] + noise * data_ref[:, 0, :]
    out_ref[:, 1, :] = total[:, 64:128] + noise * data_ref[:, 1, :]


def exchange(x, axes):
    return lax.all_to_all(x, axes, 0, 0, tiled=True)


def shards(data_vec, kernel, time_spectrum, prior_spectrum, noise_var):
    table = jnp.asarray(fourier_table(2, 16))
    rows = sine_matrix(128)
    order = row_order()
    forward = jnp.asarray(np.concatenate(split_table(rows[:, order]), axis=1))
    high, low = split_table(rows[order].reshape(8, 16, 128))
    upper = np.concatenate([high, high], axis=2)
    lower = np.concatenate([low, np.zeros_like(low)], axis=2)
    backward = jnp.asarray(np.concatenate([upper, lower], axis=1))
    columns = [jnp.asarray(t) for t in split_table(np.kron(np.eye(2), sine_matrix(64)))]

    spread = call(
        spread_body,
        jax.ShapeDtypeStruct((64, 128), f32),
        (data_vec,),
        (whole(),),
        hint=2e10,
    )
    by_time = exchange(spread.reshape(16, 4, 128), ("z", "core")).reshape(64, 128)
    spectra = call(
        spectra_body,
        jax.ShapeDtypeStruct((2, 8, 8, 128), f32),
        (by_time, table),
        (whole(), whole()),
        hint=2e10,
    )
    gathered = exchange(spectra.reshape(16, 8, 128), ("x_hi", "stripe"))
    grids = call(
        adjoint_body,
        jax.ShapeDtypeStruct((8, 16, 1024), bf16),
        (gathered.reshape(2, 8, 8, 128), kernel, time_spectrum.reshape(1, 4), *columns),
        (whole(),) * 5,
        (pltpu.VMEM((128, 128), f32),),
        limit=20 << 20,
    )
    grids = exchange(grids, "stripe").reshape(128, 1024)
    images = call(
        images_body,
        jax.ShapeDtypeStruct((4, 8, 8, 128), bf16),
        (grids, kernel, prior_spectrum.T, forward, backward, *columns),
        (whole(),) * 7,
        (pltpu.VMEM((128, 128), f32), pltpu.VMEM((1024, 1536), bf16)),
        limit=20 << 20,
    )
    images = exchange(images.reshape(32, 8, 128), ("x_hi", "core", "stripe"))
    sums = call(
        times_body,
        jax.ShapeDtypeStruct((32, 128), f32),
        (images.reshape(4, 8, 8, 128), jnp.asarray(inverse_table())),
        (whole(), whole()),
    )
    sums = exchange(sums.reshape(8, 4, 128), "z").reshape(32, 128)
    return call(
        finish_body,
        jax.ShapeDtypeStruct((4, 2, 64), f32),
        (sums, data_vec, noise_var.reshape(1, 64)),
        (whole(),) * 3,
    )


def solution(mesh):
    fine = Mesh(mesh.devices.reshape(2, 8, 2, 8), ("x_hi", "z", "core", "stripe"))
    tm = ("x_hi", "z", "core")
    return jax.shard_map(
        shards,
        mesh=fine,
        in_specs=(
            P(tm, None, "stripe"),
            P(tm, None, None, "stripe"),
            P(tm),
            P(),
            P("stripe"),
        ),
        out_specs=P(tm, None, "stripe"),
        check_vma=False,
    )
```

```python
import math

import jax
import jax.numpy as jnp
import numpy as np
from jax import lax
from jax.experimental import pallas as pl
from jax.experimental.pallas import tpu as pltpu
from jax.sharding import Mesh
from jax.sharding import PartitionSpec as P

f32 = jnp.float32
bf16 = jnp.bfloat16


def whole():
    return pl.BlockSpec(memory_space=pltpu.VMEM)


def call(body, out_shape, operands, specs, scratch=(), limit=4 << 20, hint=1e6):
    return pl.pallas_call(
        body,
        out_shape=out_shape,
        in_specs=list(specs),
        out_specs=whole(),
        scratch_shapes=list(scratch),
        cost_estimate=pl.CostEstimate(
            flops=int(hint), transcendentals=0, bytes_accessed=100_000
        ),
        compiler_params=pltpu.CompilerParams(vmem_limit_bytes=limit),
    )(*operands)


def mm(a, b, dims=((1,), (0,))):
    return lax.dot_general(
        a, b, (dims, ((), ())), preferred_element_type=f32
    )


def fourier_table(halves, blocks):
    steps = np.arange(128)
    angles = np.outer(steps, steps) % 256 * (math.pi / 128)
    pair = np.stack([np.cos(angles), -np.sin(angles)]) / math.sqrt(128)
    pair = pair.reshape(2, halves, blocks, 4, halves, 64).transpose(4, 2, 1, 0, 3, 5)
    return triple_table(pair.reshape(halves, blocks, halves * 8, 64))


def inverse_table():
    steps = np.arange(128)
    angles = np.outer(steps, steps) % 256 * (math.pi / 128)
    pair = np.stack([np.cos(angles), -np.sin(angles)]) / math.sqrt(128)
    pair = pair.reshape(2, 2, 8, 2, 4, 2, 8, 2, 4)
    pair = pair.transpose(2, 5, 7, 6, 8, 1, 3, 0, 4)
    return triple_table(pair.reshape(8, 4, 32, 32))


def sine_matrix(length):
    numbers = np.arange(length) + 1
    product = np.outer(numbers, numbers) % (2 * (length + 1))
    return np.sin(product * (math.pi / (length + 1))) * math.sqrt(2.0 / (length + 1))


def row_order():
    stripe, parity, c = np.meshgrid(np.arange(8), np.arange(2), np.arange(8), indexing="ij")
    return (stripe * 16 + 2 * c + parity).reshape(-1)


def low_half(shape):
    return lax.broadcasted_iota(jnp.int32, shape, len(shape) - 1) < 64


def swap_halves(first, second):
    keep = low_half(first.shape)
    low = jnp.where(keep, first, pltpu.roll(second, 64, 1))
    high = jnp.where(keep, pltpu.roll(first, 64, 1), second)
    return low, high


def split(x):
    high = x.astype(bf16)
    return high, (x - high.astype(f32)).astype(bf16)


def split_table(x):
    high = x.astype(np.float32).astype(bf16)
    return high, (x - high.astype(np.float64)).astype(np.float32).astype(bf16)


def triple_table(x):
    high, low = split_table(x)
    return np.concatenate([high, high, low], axis=-1)


def triple_product(table, x):
    high, low = split(x)
    return mm(table, jnp.concatenate([high, low, high], axis=0))


def column_transform(x, high_ref, low_ref):
    high, low = split(x)
    both = mm(jnp.concatenate([high, low], axis=0), high_ref[...])
    return both[:128] + both[128:] + mm(high, low_ref[...])


def spread_body(data_ref, out_ref):
    flat = jnp.concatenate([data_ref[:, 0, :], data_ref[:, 1, :]], axis=1)
    two = jnp.concatenate([flat, flat], axis=0)
    for r in range(8):
        out_ref[r * 8 : r * 8 + 8, :] = two


def block_of_table(table_ref):
    return table_ref[lax.axis_index("x_hi"), lax.axis_index("z") * 2 + lax.axis_index("core")]


def spectra_body(data_ref, table_ref, out_ref):
    spectra = triple_product(block_of_table(table_ref), data_ref[...])
    for half in range(2):
        for r in range(8):
            out_ref[half, r] = spectra[half * 8 : half * 8 + 8, :]


def adjoint_body(gathered_ref, kernel_ref, scale_ref, high_ref, low_ref, out_ref, grid_ref):
    parts = [[], []]
    for j in range(4):
        first = gathered_ref[0, 2 * j] + gathered_ref[1, 2 * j]
        second = gathered_ref[0, 2 * j + 1] + gathered_ref[1, 2 * j + 1]
        low, high = swap_halves(first, second)
        parts[0].append(low)
        parts[1].append(high)
    rows = [jnp.concatenate(part, axis=1) for part in parts]
    sub = lax.broadcasted_iota(jnp.int32, (8, 512), 0)
    turned = [jnp.where(sub < 4, pltpu.roll(r, 4, 0), -pltpu.roll(r, 4, 0)) for r in rows]
    straight = jnp.concatenate(rows, axis=0)
    turned = jnp.concatenate(turned, axis=0)
    both = jnp.concatenate([straight, turned], axis=1)
    freq = lax.broadcasted_iota(jnp.int32, (16, 1024), 0) % 4
    total = None
    for k in range(4):
        left = jnp.where(freq == k, both, 0.0).astype(bf16)
        term = mm(left, kernel_ref[k].reshape(1024, 1024))
        total = term if total is None else total + term
    row = lax.broadcasted_iota(jnp.int32, (16, 128), 0) % 4
    scale = jnp.broadcast_to(scale_ref[0:1, 0:1], (16, 128))
    for k in range(1, 4):
        scale = jnp.where(row == k, scale_ref[0:1, k : k + 1], scale)
    scale = jnp.concatenate([scale] * 8, axis=1)
    total = total * scale
    stack = jnp.concatenate([total[:, c * 128 : c * 128 + 128] for c in range(8)], axis=0)
    grid_ref[...] = column_transform(stack, high_ref, low_ref)
    for m in range(8):
        first = grid_ref[pl.ds(2 * m, 8, stride=16), :]
        second = grid_ref[pl.ds(2 * m + 1, 8, stride=16), :]
        tile = jnp.concatenate(swap_halves(first, second), axis=0).astype(bf16)
        for r in range(8):
            out_ref[r, :, m * 128 : m * 128 + 128] = tile


def images_body(
    grids_ref, kernel_ref, prior_ref, forward_ref, backward_ref, high_ref, low_ref, out_ref, grid_ref, turned_ref
):
    stripe = lax.axis_index("stripe")
    for k in range(2, 4):
        for c in range(2):
            for column in range(0, 1024, 512):
                tile = kernel_ref[k, c, :, column : column + 512]
                turned_ref[k - 2, column : column + 512, c * 512 : c * 512 + 512] = tile.T
    grids = grids_ref[...]
    modes = mm(forward_ref[...], jnp.concatenate([grids, grids], axis=0))
    prior = prior_ref[...].T
    prior = jnp.concatenate([prior, prior], axis=1)
    modes = modes * jnp.concatenate([prior] * 8, axis=1)
    modes = jnp.concatenate(split(modes), axis=0)
    back = mm(backward_ref[stripe], modes)
    back = back[0:16, :] + back[16:32, :]
    for m in range(8):
        first, second = swap_halves(
            back[0:8, m * 128 : m * 128 + 128], back[8:16, m * 128 : m * 128 + 128]
        )
        grid_ref[pl.ds(2 * m, 8, stride=16), :] = first
        grid_ref[pl.ds(2 * m + 1, 8, stride=16), :] = second
    smooth = column_transform(grid_ref[...], high_ref, low_ref)
    smooth = jnp.concatenate([smooth[c * 16 : c * 16 + 16, :] for c in range(8)], axis=1)
    left = smooth.astype(bf16)
    freq = lax.broadcasted_iota(jnp.int32, (16, 1024), 0) % 4
    total = None
    for k in range(4):
        if k >= 2:
            term = mm(left, turned_ref[k - 2])
        else:
            term = None
            for c in range(4):
                right = kernel_ref[k, :, :, c * 256 : c * 256 + 256].reshape(1024, 256)
                piece = mm(left[:, c * 256 : c * 256 + 256], right, ((1,), (1,)))
                term = piece if term is None else term + piece
        total = term if k == 0 else jnp.where(freq == k, term, total)
    sub = lax.broadcasted_iota(jnp.int32, (8, 512), 0)
    rows = []
    for n in range(2):
        moved = pltpu.roll(total[n * 8 : n * 8 + 8, 512:], 4, 0)
        rows.append(total[n * 8 : n * 8 + 8, :512] + jnp.where(sub < 4, -moved, moved))
    total = jnp.concatenate(rows, axis=0)
    for j in range(4):
        low, high = swap_halves(
            total[0:8, j * 128 : j * 128 + 128], total[8:16, j * 128 : j * 128 + 128]
        )
        low, high = low.astype(bf16), high.astype(bf16)
        for copy in range(4):
            out_ref[copy, 2 * j] = low
            out_ref[copy, 2 * j + 1] = high


def times_body(images_ref, table_ref, out_ref):
    half = lax.axis_index("x_hi") * 2 + lax.axis_index("core")
    blocks = []
    for block in range(4):
        total = images_ref[block, 0].astype(f32)
        for r in range(1, 8):
            total = total + images_ref[block, r].astype(f32)
        blocks.append(total)
    images = jnp.concatenate(blocks, axis=0)
    table = table_ref[lax.axis_index("z"), half]
    out_ref[...] = triple_product(table, images)


def finish_body(sums_ref, data_ref, noise_ref, out_ref):
    total = sums_ref[0:8, :]
    for r in range(1, 4):
        total = total + sums_ref[r * 8 : r * 8 + 8, :]
    total = total[0:4, :] + total[4:8, :]
    noise = noise_ref[...]
    out_ref[:, 0, :] = total[:, 0:64] + noise * data_ref[:, 0, :]
    out_ref[:, 1, :] = total[:, 64:128] + noise * data_ref[:, 1, :]


def exchange(x, axes):
    return lax.all_to_all(x, axes, 0, 0, tiled=True)


def shards(data_vec, kernel, time_spectrum, prior_spectrum, noise_var):
    table = jnp.asarray(fourier_table(2, 16))
    rows = sine_matrix(128)
    order = row_order()
    forward = jnp.asarray(np.concatenate(split_table(rows[:, order]), axis=1))
    high, low = split_table(rows[order].reshape(8, 16, 128))
    upper = np.concatenate([high, high], axis=2)
    lower = np.concatenate([low, np.zeros_like(low)], axis=2)
    backward = jnp.asarray(np.concatenate([upper, lower], axis=1))
    columns = [jnp.asarray(t) for t in split_table(np.kron(np.eye(2), sine_matrix(64)))]

    spread = call(
        spread_body,
        jax.ShapeDtypeStruct((64, 128), f32),
        (data_vec,),
        (whole(),),
        hint=2e10,
    )
    by_time = exchange(spread.reshape(16, 4, 128), ("z", "core")).reshape(64, 128)
    spectra = call(
        spectra_body,
        jax.ShapeDtypeStruct((2, 8, 8, 128), f32),
        (by_time, table),
        (whole(), whole()),
        hint=2e10,
    )
    gathered = exchange(spectra.reshape(16, 8, 128), ("x_hi", "stripe"))
    grids = call(
        adjoint_body,
        jax.ShapeDtypeStruct((8, 16, 1024), bf16),
        (gathered.reshape(2, 8, 8, 128), kernel, time_spectrum.reshape(1, 4), *columns),
        (whole(),) * 5,
        (pltpu.VMEM((128, 128), f32),),
        limit=20 << 20,
    )
    grids = exchange(grids, "stripe").reshape(128, 1024)
    images = call(
        images_body,
        jax.ShapeDtypeStruct((4, 8, 8, 128), bf16),
        (grids, kernel, prior_spectrum.T, forward, backward, *columns),
        (whole(),) * 7,
        (pltpu.VMEM((128, 128), f32), pltpu.VMEM((2, 1024, 1024), bf16)),
        limit=20 << 20,
    )
    images = exchange(images.reshape(32, 8, 128), ("x_hi", "core", "stripe"))
    sums = call(
        times_body,
        jax.ShapeDtypeStruct((32, 128), f32),
        (images.reshape(4, 8, 8, 128), jnp.asarray(inverse_table())),
        (whole(), whole()),
    )
    sums = exchange(sums.reshape(8, 4, 128), "z").reshape(32, 128)
    return call(
        finish_body,
        jax.ShapeDtypeStruct((4, 2, 64), f32),
        (sums, data_vec, noise_var.reshape(1, 64)),
        (whole(),) * 3,
    )


def solution(mesh):
    fine = Mesh(mesh.devices.reshape(2, 8, 2, 8), ("x_hi", "z", "core", "stripe"))
    tm = ("x_hi", "z", "core")
    return jax.shard_map(
        shards,
        mesh=fine,
        in_specs=(
            P(tm, None, "stripe"),
            P(tm, None, None, "stripe"),
            P(tm),
            P(),
            P("stripe"),
        ),
        out_specs=P(tm, None, "stripe"),
        check_vma=False,
    )
```

```python
import math

import jax
import jax.numpy as jnp
import numpy as np
from jax import lax
from jax.experimental import pallas as pl
from jax.experimental.pallas import tpu as pltpu
from jax.sharding import Mesh
from jax.sharding import PartitionSpec as P

f32 = jnp.float32
bf16 = jnp.bfloat16


def whole():
    return pl.BlockSpec(memory_space=pltpu.VMEM)


def call(body, out_shape, operands, specs, scratch=(), limit=4 << 20, hint=1e6):
    return pl.pallas_call(
        body,
        out_shape=out_shape,
        in_specs=list(specs),
        out_specs=whole(),
        scratch_shapes=list(scratch),
        cost_estimate=pl.CostEstimate(
            flops=int(hint), transcendentals=0, bytes_accessed=100_000
        ),
        compiler_params=pltpu.CompilerParams(vmem_limit_bytes=limit),
    )(*operands)


def mm(a, b, dims=((1,), (0,))):
    return lax.dot_general(
        a, b, (dims, ((), ())), preferred_element_type=f32
    )


def fourier_table(halves, blocks):
    steps = np.arange(128)
    angles = np.outer(steps, steps) % 256 * (math.pi / 128)
    pair = np.stack([np.cos(angles), -np.sin(angles)]) / math.sqrt(128)
    pair = pair.reshape(2, halves, blocks, 4, halves, 64).transpose(4, 2, 1, 0, 3, 5)
    return triple_table(pair.reshape(halves, blocks, halves * 8, 64))


def inverse_table():
    steps = np.arange(128)
    angles = np.outer(steps, steps) % 256 * (math.pi / 128)
    pair = np.stack([np.cos(angles), -np.sin(angles)]) / math.sqrt(128)
    pair = pair.reshape(2, 2, 8, 2, 4, 2, 8, 2, 4)
    pair = pair.transpose(2, 5, 7, 6, 8, 1, 3, 0, 4)
    return triple_table(pair.reshape(8, 4, 32, 32))


def sine_matrix(length):
    numbers = np.arange(length) + 1
    product = np.outer(numbers, numbers) % (2 * (length + 1))
    return np.sin(product * (math.pi / (length + 1))) * math.sqrt(2.0 / (length + 1))


def row_order():
    stripe, parity, c = np.meshgrid(np.arange(8), np.arange(2), np.arange(8), indexing="ij")
    return (stripe * 16 + 2 * c + parity).reshape(-1)


def low_half(shape):
    return lax.broadcasted_iota(jnp.int32, shape, len(shape) - 1) < 64


def swap_halves(first, second):
    keep = low_half(first.shape)
    low = jnp.where(keep, first, pltpu.roll(second, 64, 1))
    high = jnp.where(keep, pltpu.roll(first, 64, 1), second)
    return low, high


def split(x):
    high = x.astype(bf16)
    return high, (x - high.astype(f32)).astype(bf16)


def split_table(x):
    high = x.astype(np.float32).astype(bf16)
    return high, (x - high.astype(np.float64)).astype(np.float32).astype(bf16)


def triple_table(x):
    high, low = split_table(x)
    return np.concatenate([high, high, low], axis=-1)


def triple_product(table, x):
    high, low = split(x)
    return mm(table, jnp.concatenate([high, low, high], axis=0))


def column_transform(x, high_ref, low_ref):
    high, low = split(x)
    both = mm(jnp.concatenate([high, low], axis=0), high_ref[...])
    return both[:128] + both[128:] + mm(high, low_ref[...])


def spread_body(data_ref, out_ref):
    flat = jnp.concatenate([data_ref[:, 0, :], data_ref[:, 1, :]], axis=1)
    two = jnp.concatenate([flat, flat], axis=0)
    for r in range(8):
        out_ref[r * 8 : r * 8 + 8, :] = two


def block_of_table(table_ref):
    return table_ref[lax.axis_index("x_hi"), lax.axis_index("z") * 2 + lax.axis_index("core")]


def spectra_body(data_ref, table_ref, out_ref):
    spectra = triple_product(block_of_table(table_ref), data_ref[...])
    for half in range(2):
        for r in range(8):
            out_ref[half, r] = spectra[half * 8 : half * 8 + 8, :]


def adjoint_body(gathered_ref, kernel_ref, scale_ref, high_ref, low_ref, out_ref, grid_ref):
    parts = [[], []]
    for j in range(4):
        first = gathered_ref[0, 2 * j] + gathered_ref[1, 2 * j]
        second = gathered_ref[0, 2 * j + 1] + gathered_ref[1, 2 * j + 1]
        low, high = swap_halves(first, second)
        parts[0].append(low)
        parts[1].append(high)
    rows = [jnp.concatenate(part, axis=1) for part in parts]
    sub = lax.broadcasted_iota(jnp.int32, (8, 512), 0)
    turned = [jnp.where(sub < 4, pltpu.roll(r, 4, 0), -pltpu.roll(r, 4, 0)) for r in rows]
    straight = jnp.concatenate(rows, axis=0)
    turned = jnp.concatenate(turned, axis=0)
    both = jnp.concatenate([straight, turned], axis=1)
    freq = lax.broadcasted_iota(jnp.int32, (16, 1024), 0) % 4
    total = None
    for k in range(4):
        left = jnp.where(freq == k, both, 0.0).astype(bf16)
        term = mm(left, kernel_ref[k].reshape(1024, 1024))
        total = term if total is None else total + term
    row = lax.broadcasted_iota(jnp.int32, (16, 128), 0) % 4
    scale = jnp.broadcast_to(scale_ref[0:1, 0:1], (16, 128))
    for k in range(1, 4):
        scale = jnp.where(row == k, scale_ref[0:1, k : k + 1], scale)
    scale = jnp.concatenate([scale] * 8, axis=1)
    total = total * scale
    stack = jnp.concatenate([total[:, c * 128 : c * 128 + 128] for c in range(8)], axis=0)
    grid_ref[...] = column_transform(stack, high_ref, low_ref)
    for m in range(8):
        first = grid_ref[pl.ds(2 * m, 8, stride=16), :]
        second = grid_ref[pl.ds(2 * m + 1, 8, stride=16), :]
        tile = jnp.concatenate(swap_halves(first, second), axis=0).astype(bf16)
        for r in range(8):
            out_ref[r, :, m * 128 : m * 128 + 128] = tile


def images_body(
    grids_ref, kernel_ref, prior_ref, forward_ref, backward_ref, high_ref, low_ref, out_ref, grid_ref, turned_ref
):
    stripe = lax.axis_index("stripe")
    for k in range(1, 4):
        for c in range(2):
            for column in range(0, 1024, 512):
                tile = kernel_ref[k, c, :, column : column + 512]
                turned_ref[k - 1, column : column + 512, c * 512 : c * 512 + 512] = tile.T
    grids = grids_ref[...]
    modes = mm(forward_ref[...], jnp.concatenate([grids, grids], axis=0))
    prior = prior_ref[...].T
    prior = jnp.concatenate([prior, prior], axis=1)
    modes = modes * jnp.concatenate([prior] * 8, axis=1)
    modes = jnp.concatenate(split(modes), axis=0)
    back = mm(backward_ref[stripe], modes)
    back = back[0:16, :] + back[16:32, :]
    for m in range(8):
        first, second = swap_halves(
            back[0:8, m * 128 : m * 128 + 128], back[8:16, m * 128 : m * 128 + 128]
        )
        grid_ref[pl.ds(2 * m, 8, stride=16), :] = first
        grid_ref[pl.ds(2 * m + 1, 8, stride=16), :] = second
    smooth = column_transform(grid_ref[...], high_ref, low_ref)
    smooth = jnp.concatenate([smooth[c * 16 : c * 16 + 16, :] for c in range(8)], axis=1)
    left = smooth.astype(bf16)
    freq = lax.broadcasted_iota(jnp.int32, (16, 1024), 0) % 4
    total = None
    for k in range(4):
        if k >= 1:
            term = mm(left, turned_ref[k - 1])
        else:
            term = None
            for c in range(4):
                right = kernel_ref[k, :, :, c * 256 : c * 256 + 256].reshape(1024, 256)
                piece = mm(left[:, c * 256 : c * 256 + 256], right, ((1,), (1,)))
                term = piece if term is None else term + piece
        total = term if k == 0 else jnp.where(freq == k, term, total)
    sub = lax.broadcasted_iota(jnp.int32, (8, 512), 0)
    rows = []
    for n in range(2):
        moved = pltpu.roll(total[n * 8 : n * 8 + 8, 512:], 4, 0)
        rows.append(total[n * 8 : n * 8 + 8, :512] + jnp.where(sub < 4, -moved, moved))
    total = jnp.concatenate(rows, axis=0)
    for j in range(4):
        low, high = swap_halves(
            total[0:8, j * 128 : j * 128 + 128], total[8:16, j * 128 : j * 128 + 128]
        )
        low, high = low.astype(bf16), high.astype(bf16)
        for copy in range(4):
            out_ref[copy, 2 * j] = low
            out_ref[copy, 2 * j + 1] = high


def times_body(images_ref, table_ref, out_ref):
    half = lax.axis_index("x_hi") * 2 + lax.axis_index("core")
    blocks = []
    for block in range(4):
        total = images_ref[block, 0].astype(f32)
        for r in range(1, 8):
            total = total + images_ref[block, r].astype(f32)
        blocks.append(total)
    images = jnp.concatenate(blocks, axis=0)
    table = table_ref[lax.axis_index("z"), half]
    out_ref[...] = triple_product(table, images)


def finish_body(sums_ref, data_ref, noise_ref, out_ref):
    total = sums_ref[0:8, :]
    for r in range(1, 4):
        total = total + sums_ref[r * 8 : r * 8 + 8, :]
    total = total[0:4, :] + total[4:8, :]
    noise = noise_ref[...]
    out_ref[:, 0, :] = total[:, 0:64] + noise * data_ref[:, 0, :]
    out_ref[:, 1, :] = total[:, 64:128] + noise * data_ref[:, 1, :]


def exchange(x, axes):
    return lax.all_to_all(x, axes, 0, 0, tiled=True)


def shards(data_vec, kernel, time_spectrum, prior_spectrum, noise_var):
    table = jnp.asarray(fourier_table(2, 16))
    rows = sine_matrix(128)
    order = row_order()
    forward = jnp.asarray(np.concatenate(split_table(rows[:, order]), axis=1))
    high, low = split_table(rows[order].reshape(8, 16, 128))
    upper = np.concatenate([high, high], axis=2)
    lower = np.concatenate([low, np.zeros_like(low)], axis=2)
    backward = jnp.asarray(np.concatenate([upper, lower], axis=1))
    columns = [jnp.asarray(t) for t in split_table(np.kron(np.eye(2), sine_matrix(64)))]

    spread = call(
        spread_body,
        jax.ShapeDtypeStruct((64, 128), f32),
        (data_vec,),
        (whole(),),
        hint=2e10,
    )
    by_time = exchange(spread.reshape(16, 4, 128), ("z", "core")).reshape(64, 128)
    spectra = call(
        spectra_body,
        jax.ShapeDtypeStruct((2, 8, 8, 128), f32),
        (by_time, table),
        (whole(), whole()),
        hint=2e10,
    )
    gathered = exchange(spectra.reshape(16, 8, 128), ("x_hi", "stripe"))
    grids = call(
        adjoint_body,
        jax.ShapeDtypeStruct((8, 16, 1024), bf16),
        (gathered.reshape(2, 8, 8, 128), kernel, time_spectrum.reshape(1, 4), *columns),
        (whole(),) * 5,
        (pltpu.VMEM((128, 128), f32),),
        limit=20 << 20,
    )
    grids = exchange(grids, "stripe").reshape(128, 1024)
    images = call(
        images_body,
        jax.ShapeDtypeStruct((4, 8, 8, 128), bf16),
        (grids, kernel, prior_spectrum.T, forward, backward, *columns),
        (whole(),) * 7,
        (pltpu.VMEM((128, 128), f32), pltpu.VMEM((3, 1024, 1024), bf16)),
        limit=20 << 20,
    )
    images = exchange(images.reshape(32, 8, 128), ("x_hi", "core", "stripe"))
    sums = call(
        times_body,
        jax.ShapeDtypeStruct((32, 128), f32),
        (images.reshape(4, 8, 8, 128), jnp.asarray(inverse_table())),
        (whole(), whole()),
    )
    sums = exchange(sums.reshape(8, 4, 128), "z").reshape(32, 128)
    return call(
        finish_body,
        jax.ShapeDtypeStruct((4, 2, 64), f32),
        (sums, data_vec, noise_var.reshape(1, 64)),
        (whole(),) * 3,
    )


def solution(mesh):
    fine = Mesh(mesh.devices.reshape(2, 8, 2, 8), ("x_hi", "z", "core", "stripe"))
    tm = ("x_hi", "z", "core")
    return jax.shard_map(
        shards,
        mesh=fine,
        in_specs=(
            P(tm, None, "stripe"),
            P(tm, None, None, "stripe"),
            P(tm),
            P(),
            P("stripe"),
        ),
        out_specs=P(tm, None, "stripe"),
        check_vma=False,
    )
```
